32 devices in a mesh: grp: 2 (over y), date: 4 (over x, core), strip: 4 (over z).
Axes of the slice: x: 2, y: 2, z: 4, core: 2. Of those that a mesh axis runs over, the one named last changes fastest.
Arguments:
- acquisitions: bfloat16 [16, 64, 2, 16384], P(('grp', 'date'), 'strip'), parts along dimension 0, may hold values from -22 to 22
- partners: int32 [2, 16], P(None, ('grp', 'date')), parts along dimension 1, may hold values from 0 to 7, as said below
- band_shifts: int32 [2, 16], P(None, ('grp', 'date')), parts along dimension 1, may hold values from -24 to 24
Outputs:
- interferograms: bfloat16 [2, 16, 2, 64, 4096], P(None, ('grp', 'date'), None, 'strip'), parts along dimension 1
- coherence: bfloat16 [2, 16, 64, 4096], P(None, ('grp', 'date'), 'strip'), parts along dimension 1
The draws below stay inside these ranges and needn't reach their ends.
There are 2 independent parts, one for each index of `grp`. The reference program is written for one: setup_inputs(seed, part) draws one part's arguments, and reference() takes and returns one part's arrays. A program takes and returns all parts, laid end to end along the dimension named above; each array names one. Nothing has to cross between parts.
Inputs may be any that keep to these rules, and one draw needn't show every extreme that they name: For each matching m and each date group g (dates g * 2 to (g + 1) * 2 - 1), the partners of the group's dates are the 2 different dates of one other group: g with its lowest bit flipped for m = 0, and (g + 2) modulo 4 for m = 1.
All inputs are finite; a program needn't handle non-finite values.
Results may differ from the reference program's by a relative error of at most 0.0075.
Values may be sent and summed in bfloat16 or wider, within the bound.
A program may use at most 64 MiB of HBM per device.

```python
import math
import jax
import jax.numpy as jnp
from jax import lax

RG = 16384
DATE_DEV = 2
NDATES = 8
AZ = 64


def draw_acquisitions(key, part):
    scene = jnp.clip(jax.random.normal(jax.random.fold_in(key, 11), (AZ, 2, RG), jnp.float32), -5.0, 5.0)
    levels = jax.random.uniform(jax.random.fold_in(key, 12), (NDATES,), jnp.float32, 0.3, 0.9)
    noise = jnp.clip(jax.random.normal(jax.random.fold_in(key, 13), (NDATES, AZ, 2, RG), jnp.float32), -5.0, 5.0)
    mixed = levels[:, None, None, None] * scene[None] + jnp.sqrt(1.0 - levels * levels)[:, None, None, None] * noise
    return mixed.astype(jnp.bfloat16)


def draw_partners(key, part):
    groups = NDATES // DATE_DEV
    scores = jax.random.randint(jax.random.fold_in(key, 21), (2, groups, DATE_DEV), 0, 1 << 20) * DATE_DEV + jnp.arange(DATE_DEV, dtype=jnp.int32)
    slot_order = jnp.argsort(scores, axis=2, stable=True).astype(jnp.int32)
    home = jnp.arange(groups, dtype=jnp.int32)
    nearby = home + 1 - 2 * (home % 2)
    faraway = (home + groups // 2) % groups
    target = jnp.stack([nearby, faraway])
    return (target[:, :, None] * DATE_DEV + slot_order).reshape(2, NDATES)


def place_ends(values, stream_key, low, high):
    longest = values.shape.index(max(values.shape))
    spots = []
    for shift in (0, 1):
        where = [jax.random.randint(jax.random.fold_in(stream_key, axis), (), 0, length) for axis, length in enumerate(values.shape)]
        where[longest] = (where[longest] + shift) % values.shape[longest]
        spots.append(tuple(where))
    return values.at[spots[0]].set(low).at[spots[1]].set(high)


def setup_inputs(seed: int = 0, part: int = 0) -> dict:
    streams_of = jax.random.split(jax.random.key(seed), 4)
    part_splits = jax.random.split(jax.random.fold_in(streams_of[3], part), 4)
    return {
        "acquisitions": draw_acquisitions(jax.random.fold_in(jax.random.fold_in(streams_of[3], part), 71), part),
        "partners": draw_partners(jax.random.fold_in(jax.random.fold_in(streams_of[3], part), 71), part),
        "band_shifts": place_ends(jax.random.randint(part_splits[2], (2, NDATES), -24, 25), jax.random.fold_in(part_splits[2], 1), -24, 24).astype(jnp.int32),
    }


band_width = 0.8
bin_count = 256.0
epsilon = 1e-06

def make_taps(shift_bin):
    positions = jnp.arange(64, dtype=jnp.float32)
    centred = positions - 31.5
    hamming = 0.54 - 0.46 * jnp.cos(2.0 * math.pi * positions / 63.0)
    lowpass = hamming * band_width * jnp.sinc(band_width * centred)
    angles = 2.0 * math.pi * shift_bin.astype(jnp.float32) * centred / bin_count
    return ((lowpass * jnp.cos(angles)).astype(jnp.bfloat16), (lowpass * jnp.sin(angles)).astype(jnp.bfloat16))

def band_filter(image_rows, taps_real, taps_imag):
    signal = image_rows[:, 0, :].astype(jnp.float32) + 1j * image_rows[:, 1, :].astype(jnp.float32)
    padded = jnp.pad(signal, ((0, 0), (32, 31)))
    kernel = (taps_real.astype(jnp.float32) + 1j * taps_imag.astype(jnp.float32))[::-1]
    length = 1 << (RG + 126).bit_length()
    spectrum = jnp.fft.fft(padded, length, axis=1) * jnp.fft.fft(kernel, length)[None, :]
    result = jnp.fft.ifft(spectrum, axis=1)[:, 63:63 + RG]
    return jnp.stack([jnp.real(result), jnp.imag(result)], axis=1).astype(jnp.bfloat16)

def range_looks(values):
    return values.reshape(values.shape[0], values.shape[1] // 4, 4).sum(axis=2)

def look_sums(first_band, second_band):
    first_real = first_band[:, 0].astype(jnp.float32)
    first_imag = first_band[:, 1].astype(jnp.float32)
    second_real = second_band[:, 0].astype(jnp.float32)
    second_imag = second_band[:, 1].astype(jnp.float32)
    return jnp.stack([range_looks(first_real * second_real + first_imag * second_imag), range_looks(first_imag * second_real - first_real * second_imag), range_looks(first_real * first_real + first_imag * first_imag), range_looks(second_real * second_real + second_imag * second_imag)])

def azimuth_window(framed, row_count):
    running = framed[:, 0:row_count]
    for offset in range(1, 20):
        running = running + framed[:, offset:offset + row_count]
    return running

def finish(window):
    mean_cross = (window[0:2] / 80.0).astype(jnp.bfloat16)
    magnitude = jnp.sqrt(window[0] * window[0] + window[1] * window[1])
    coherent = (magnitude / jnp.sqrt(window[2] * window[3] + epsilon)).astype(jnp.bfloat16)
    return (mean_cross, coherent)

def reference(acquisitions, partners, band_shifts):
    date_index = jnp.arange(NDATES, dtype=jnp.int32)
    cross_list = []
    coherence_list = []
    for match_index in range(2):

        def one_pair(pair_entry):
            own_date, other_date, shift_bin = pair_entry
            first_rows = lax.dynamic_index_in_dim(acquisitions, own_date, 0, keepdims=False)
            second_rows = lax.dynamic_index_in_dim(acquisitions, other_date, 0, keepdims=False)
            taps_real, taps_imag = make_taps(shift_bin)
            look_terms = look_sums(band_filter(first_rows, taps_real, taps_imag), band_filter(second_rows, taps_real, taps_imag))
            framed = jnp.pad(look_terms, ((0, 0), (10, 10), (0, 0)))
            return finish(azimuth_window(framed, look_terms.shape[1]))
        mean_cross, coherent = lax.map(one_pair, (date_index, partners[match_index].astype(jnp.int32), band_shifts[match_index]))
        cross_list.append(mean_cross)
        coherence_list.append(coherent)
    return (jnp.stack(cross_list), jnp.stack(coherence_list))
```

```python
import math

import jax
import jax.numpy as jnp
from jax import lax
from jax.experimental import pallas as pl
from jax.experimental.pallas import tpu as pltpu
from jax.sharding import PartitionSpec as P

band_width = 0.8
bin_count = 256.0
epsilon = 1e-06
below = 10
above = 9
lanes = 128
rows = 16
tiles = 8
planes = 4
lag = 3
MESH = pl.DeviceIdType.MESH


def make_taps(shifts):
    lane = lax.broadcasted_iota(jnp.int32, shifts.shape, 1)
    inside = (lane < 32) | (lane >= 96)
    positions = jnp.where(lane < 32, lane + 32, lane - 96).astype(jnp.float32)
    centred = positions - 31.5
    hamming = 0.54 - 0.46 * jnp.cos(2.0 * math.pi * positions / 63.0)
    scaled = math.pi * band_width * centred
    lowpass = jnp.where(inside, hamming * band_width * (jnp.sin(scaled) / scaled), 0.0)
    angles = 2.0 * math.pi * shifts.astype(jnp.float32) * centred / bin_count
    return [
        (lowpass * part(angles)).astype(jnp.bfloat16).astype(jnp.float32) for part in (jnp.cos, jnp.sin)
    ]


def circulant(row):
    block = jnp.broadcast_to(row, (32, lanes))
    parts = [pltpu.roll(block, phase, 1, stride=4, stride_axis=0) for phase in range(4)]
    return jnp.concatenate(parts, axis=0).T


def build_weights(taps_ref, weight_ref, spot, source):
    real_part = circulant(taps_ref[0, pl.ds(source, 1), :])
    imag_part = circulant(taps_ref[1, pl.ds(source, 1), :])
    k = lax.broadcasted_iota(jnp.int32, (lanes, lanes), 0)
    c = lax.broadcasted_iota(jnp.int32, (lanes, lanes), 1)
    t = 4 * (c & 31) + (c >> 5)
    inside = jnp.abs(k - t) < 64
    for place, mask in ((0, inside), (1, jnp.logical_not(inside))):
        re = jnp.where(mask, real_part, 0.0)
        im = jnp.where(mask, imag_part, 0.0)
        weight_ref[spot, place, 0:lanes, 0:lanes] = re.astype(jnp.bfloat16)
        weight_ref[spot, place, 0:lanes, lanes:] = im.astype(jnp.bfloat16)
        weight_ref[spot, place, lanes:, 0:lanes] = (-im).astype(jnp.bfloat16)
        weight_ref[spot, place, lanes:, lanes:] = re.astype(jnp.bfloat16)


def place_of(partners_ref, match, slot, dates):
    place = 0
    for i in range(1, dates):
        place = place + jnp.where(lax.rem(partners_ref[match, i], dates) == slot, i, 0)
    return place


def iotas(shape):
    return lax.broadcasted_iota(jnp.int32, shape, 0), lax.broadcasted_iota(jnp.int32, shape, 1)


def ones_where(mask):
    return jnp.where(mask, 1.0, 0.0).astype(jnp.bfloat16)


def exchange_kernel(
    groups, strips, partners_ref, shifts_ref, raw_hbm, made_ref,
    raw_ref, own_ref, got_ref, edge_ref, taps_ref, weight_ref, band_ref, looks_ref, window_ref,
    up_out_ref, down_out_ref, up_in_ref, down_in_ref, result_ref,
    info_out_ref, info_in_ref, info_ref, order_ref, near_ref, parts_ref, from_up_ref, from_down_ref,
    raw_sem, got_send, got_recv, halo_send, halo_recv, info_send, info_recv, info_sem,
    up_send, up_recv, down_send, down_recv, result_send, result_recv,
):
    slots = own_ref.shape[0]
    half_tiles = got_ref.shape[2] - 2
    blocks = half_tiles // tiles
    pairs = 2 * slots
    size = tiles * lanes // 4
    ups, downs = up_in_ref.shape[2], down_in_ref.shape[2]
    me = lax.axis_index("date")
    strip = lax.axis_index("strip")
    peer_near = me + 1 - 2 * lax.rem(me, 2)
    peer_far = lax.rem(me + groups // 2, groups)
    half_near = lax.rem(me, 2)
    half_far = me // (groups // 2)
    can_up = strip < strips - 1
    can_down = strip > 0

    def peer_of(match):
        return peer_near * (1 - match) + peer_far * match

    def half_of(match):
        return half_near * (1 - match) + half_far * match

    def block_of(half, step):
        return half * step + (1 - half) * (blocks - 1 - step)

    def raw_copy(half, step):
        spot = pl.ds(pl.multiple_of((half * blocks + block_of(half, step)) * 2 * tiles, 2 * tiles), 2 * tiles)
        return pltpu.make_async_copy(raw_hbm.at[:, :, spot], raw_ref.at[:, :, spot], raw_sem.at[half, step])

    def info_copy(match):
        return pltpu.make_async_remote_copy(
            src_ref=info_out_ref.at[match],
            dst_ref=info_in_ref.at[match],
            send_sem=info_send.at[match],
            recv_sem=info_recv.at[match],
            device_id={"date": peer_of(match)},
            device_id_type=MESH,
        )

    def got_copy(match, step):
        half = 1 - half_of(match)
        spot = block_of(half, step) * tiles + 1
        return pltpu.make_async_remote_copy(
            src_ref=own_ref.at[:, pl.ds(half * half_tiles + spot, tiles)],
            dst_ref=got_ref.at[match, :, pl.ds(spot, tiles)],
            send_sem=got_send.at[match, step],
            recv_sem=got_recv.at[match, step],
            device_id={"date": peer_of(match)},
            device_id_type=MESH,
        )

    def got_wait(match, step):
        spot = block_of(half_of(match), step) * tiles + 1
        return pltpu.make_async_remote_copy(
            src_ref=own_ref.at[:, pl.ds(spot, tiles)],
            dst_ref=got_ref.at[match, :, pl.ds(spot, tiles)],
            send_sem=got_send.at[match, step],
            recv_sem=got_recv.at[match, step],
            device_id={"date": peer_of(match)},
            device_id_type=MESH,
        )

    def halo_copy(match, half):
        return pltpu.make_async_remote_copy(
            src_ref=own_ref.at[:, pl.ds(half_tiles + 1 - half, 1)],
            dst_ref=got_ref.at[match, :, pl.ds((half_tiles + 1) * (1 - half), 1)],
            send_sem=halo_send.at[match],
            recv_sem=halo_recv.at[match],
            device_id={"date": peer_of(match)},
            device_id_type=MESH,
        )

    def up_copy(match, step):
        return pltpu.make_async_remote_copy(
            src_ref=up_out_ref.at[match, step],
            dst_ref=up_in_ref.at[match, step],
            send_sem=up_send.at[match, step],
            recv_sem=up_recv.at[match, step],
            device_id={"strip": strip + 1},
            device_id_type=MESH,
        )

    def down_copy(match, step):
        return pltpu.make_async_remote_copy(
            src_ref=down_out_ref.at[match, step],
            dst_ref=down_in_ref.at[match, step],
            send_sem=down_send.at[match, step],
            recv_sem=down_recv.at[match, step],
            device_id={"strip": strip - 1},
            device_id_type=MESH,
        )

    def columns_of(half, step):
        return pl.ds(pl.multiple_of((half * blocks + block_of(half, step)) * size, size), size)

    def result_copy(match, step, half):
        return pltpu.make_async_remote_copy(
            src_ref=result_ref.at[match, step],
            dst_ref=made_ref.at[match, :, :, :, columns_of(half, step)],
            send_sem=result_send.at[match, step],
            recv_sem=result_recv.at[match, step],
            device_id={"date": peer_of(match)},
            device_id_type=MESH,
        )

    def start_raw(step, carry):
        raw_copy(1 - half_far, step).start()
        raw_copy(half_far, step).start()
        return carry

    lax.fori_loop(0, blocks, start_raw, 0)

    barrier = pltpu.get_barrier_semaphore()
    for peer in (peer_near, peer_far):
        pl.semaphore_signal(barrier, inc=1, device_id={"date": peer}, device_id_type=MESH)

    @pl.when(can_up)
    def _():
        pl.semaphore_signal(barrier, inc=1, device_id={"strip": strip + 1}, device_id_type=MESH)

    @pl.when(can_down)
    def _():
        pl.semaphore_signal(barrier, inc=1, device_id={"strip": strip - 1}, device_id_type=MESH)

    info_row = lax.broadcasted_iota(jnp.int32, (8, lanes), 0)
    for match in range(2):
        info = jnp.zeros((8, lanes), jnp.int32)
        for d in range(slots):
            info = jnp.where(info_row == d, shifts_ref[match, d], info)
            info = jnp.where(info_row == slots + d, lax.rem(partners_ref[match, d], slots), info)
        info_out_ref[match] = info

    wide = 2 * lanes
    i, j = iotas((wide, wide))
    order_ref[...] = ones_where((i & 15) == (j >> 4)) * ones_where(((i >> 5) == ((j >> 1) & 7)) & (((i >> 4) & 1) == (j & 1)))

    zero_tile = jnp.zeros((slots, 1, rows, wide), jnp.bfloat16)
    own_ref[:, pl.ds(0, 1)] = zero_tile
    own_ref[:, pl.ds(2 * half_tiles + 1, 1)] = zero_tile
    for match in range(2):
        got_ref[match, :, pl.ds((half_tiles + 1) * half_of(match), 1)] = zero_tile

    pl.semaphore_wait(barrier, 2 + can_up.astype(jnp.int32) + can_down.astype(jnp.int32))
    for match in range(2):
        info_copy(match).start()

    def prepare(half, step):
        raw_copy(half, step).wait()
        block = half * blocks + block_of(half, step)
        spot = pl.ds(pl.multiple_of(block * 2 * tiles, 2 * tiles), 2 * tiles)
        images = [raw_ref[d, :, spot].reshape(wide, lanes) for d in range(slots)]
        turned = jnp.dot(
            order_ref[...], jnp.concatenate(images, axis=1), preferred_element_type=jnp.float32
        ).astype(jnp.bfloat16)
        for d in range(slots):
            for q in range(tiles):
                for part in range(2):
                    own_ref[d, block * tiles + 1 + q, :, part * lanes : (part + 1) * lanes] = turned[
                        (2 * q + part) * rows : (2 * q + part + 1) * rows, d * lanes : (d + 1) * lanes
                    ]

    def prepare_both(step, carry):
        prepare(1 - half_far, step)

        @pl.when(step > 0)
        def _():
            got_copy(1, step).start()

        prepare(half_far, step)

        @pl.when(step == 0)
        def _():
            for match in range(2):
                halo_copy(match, 1 - half_of(match)).start()
            got_copy(1, step).start()

        got_copy(0, step).start()
        return carry

    lax.fori_loop(0, blocks, prepare_both, 0)

    own_shifts = jnp.zeros((8, lanes), jnp.int32)
    for match in range(2):
        for d in range(slots):
            own_shifts = jnp.where(info_row == match * slots + d, shifts_ref[match, d], own_shifts)
    for part, value in enumerate(make_taps(own_shifts)):
        taps_ref[part, 0:8] = value

    def weigh_own(spot, carry):
        match = spot // slots
        slot = lax.rem(spot, slots)
        place = place_of(partners_ref, match, slot, slots)
        build_weights(taps_ref, weight_ref, match * pairs + slot, match * slots + place)
        return carry

    lax.fori_loop(0, 2 * slots, weigh_own, 0)

    @pl.when(jnp.logical_not(can_down))
    def _():
        up_in_ref[...] = jnp.zeros(up_in_ref.shape, up_in_ref.dtype)

    @pl.when(jnp.logical_not(can_up))
    def _():
        down_in_ref[...] = jnp.zeros(down_in_ref.shape, down_in_ref.dtype)

    near_ref[...] = ones_where(((i >> 4) == (j >> 4)) & (j - i <= above) & (i - j <= below))
    i, j = iotas((ups, wide))
    plane = (i * 205) >> 11
    parts_ref[0:ups] = ones_where((plane == (j >> 4)) & ((j & 15) >= i - plane * below + rows - below))
    i, j = iotas((downs, wide))
    plane = (i * 57) >> 9
    parts_ref[ups:] = ones_where((plane == (j >> 4)) & ((j & 15) <= i - plane * above))
    i, j = iotas((wide, ups))
    from_up_ref[...] = ones_where(((i & 15) < below) & (j == (i >> 4) * below + (i & 15)))
    i, j = iotas((wide, downs))
    from_down_ref[...] = ones_where(
        ((i & 15) >= rows - above) & (j == (i >> 4) * above + (i & 15) - (rows - above))
    )

    for match in range(2):
        info_copy(match).wait_recv()
        copy = pltpu.make_async_copy(info_in_ref.at[match], info_ref.at[match], info_sem.at[match])
        copy.start()
        copy.wait()
    peer_shifts = jnp.zeros((8, lanes), jnp.int32)
    for match in range(2):
        for d in range(slots):
            peer_shifts = jnp.where(
                info_row == match * slots + d, jnp.broadcast_to(info_in_ref[match, d : d + 1], (8, lanes)), peer_shifts
            )
    for part, value in enumerate(make_taps(peer_shifts)):
        taps_ref[part, 8:16] = value

    def weigh_peer(spot, carry):
        match = spot // slots
        slot = lax.rem(spot, slots)
        build_weights(taps_ref, weight_ref, match * pairs + slots + slot, 8 + spot)
        return carry

    lax.fori_loop(0, 2 * slots, weigh_peer, 0)

    lane = lax.broadcasted_iota(jnp.int32, (rows, wide), 1) & (lanes - 1)
    from_before = ones_where(lane >= 64)
    from_after = ones_where(lane < 64)

    group = lax.broadcasted_iota(jnp.int32, (rows, lanes), 1) >> 5
    outer = (group == 0) | (group == 3)
    lower = group < 2
    even = (group & 1) == 0

    def pool(v):
        a = jnp.where(outer, v[0], v[2]) + pltpu.roll(jnp.where(outer, v[2], v[0]), 64, 1)
        b = jnp.where(lower, v[1], v[3]) + pltpu.roll(jnp.where(lower, v[3], v[1]), 64, 1)
        return jnp.where(even, a, b) + pltpu.roll(jnp.where(even, b, a), 32, 1)

    def compute(match, step):
        half = half_of(match)
        block = block_of(half, step)
        got_base = block * tiles + 1
        own_base = half * half_tiles + got_base

        @pl.when(step == 0)
        def _():
            halo_copy(match, half).wait_recv()
            got_wait(match, step).wait_recv()

        @pl.when(step < blocks - 1)
        def _():
            got_wait(match, step + 1).wait_recv()

        for d in range(slots):
            for q in range(tiles):
                edge_ref[d, q] = (
                    own_ref[d, own_base + q - 1] * from_before + own_ref[d, own_base + q + 1] * from_after
                )
                edge_ref[slots + d, q] = (
                    got_ref[match, d, got_base + q - 1] * from_before
                    + got_ref[match, d, got_base + q + 1] * from_after
                )

        def own_rows(d):
            return own_ref[d, pl.ds(own_base, tiles)].reshape(tiles * rows, wide)

        def got_rows(d):
            return got_ref[match, d, pl.ds(got_base, tiles)].reshape(tiles * rows, wide)

        def edge_rows(d):
            return edge_ref[d].reshape(tiles * rows, wide)

        for pair in range(pairs):
            if pair < slots:
                place = place_of(partners_ref, match, pair, slots)
                current = [own_rows(place), got_rows(pair)]
                edges = [edge_rows(place), edge_rows(slots + pair)]
            else:
                place = info_ref[match, pair, 0]
                current = [got_rows(pair - slots), own_rows(place)]
                edges = [edge_rows(pair), edge_rows(place)]
            spot = match * pairs + pair
            out = jnp.dot(
                jnp.concatenate(current, axis=0), weight_ref[spot, 0], preferred_element_type=jnp.float32
            )
            out = out + jnp.dot(
                jnp.concatenate(edges, axis=0), weight_ref[spot, 1], preferred_element_type=jnp.float32
            )
            band_ref[pair] = out
        for pair in range(pairs):
            for a in range(tiles // 4):
                sums = [[], [], [], []]
                for b in range(4):
                    top = (4 * a + b) * rows
                    fr, fi, sr, si = (
                        band_ref[pair, image * tiles * rows + top : image * tiles * rows + top + rows, part * lanes : (part + 1) * lanes]
                        for image in range(2)
                        for part in range(2)
                    )
                    sums[0].append(fr * sr + fi * si)
                    sums[1].append(fi * sr - fr * si)
                    sums[2].append(fr * fr + fi * fi)
                    sums[3].append(sr * sr + si * si)
                for p in range(planes):
                    top = (pair * planes + p) * rows
                    looks_ref[match, step, top : top + rows, a * lanes : (a + 1) * lanes] = pool(sums[p]).astype(
                        jnp.bfloat16
                    )
        parts = jnp.dot(parts_ref[...], looks_ref[match, step], preferred_element_type=jnp.float32)
        parts = parts.astype(jnp.bfloat16)

        @pl.when(can_up)
        def _():
            up_out_ref[match, step] = parts[0:ups]
            up_copy(match, step).start()

        @pl.when(can_down)
        def _():
            down_out_ref[match, step] = parts[ups:]
            down_copy(match, step).start()

    def finish(match, step):
        half = half_of(match)

        @pl.when(can_down)
        def _():
            up_copy(match, step).wait_recv()

        @pl.when(can_up)
        def _():
            down_copy(match, step).wait_recv()

        window = jnp.dot(near_ref[...], looks_ref[match, step], preferred_element_type=jnp.float32)
        window = window + jnp.dot(from_up_ref[...], up_in_ref[match, step], preferred_element_type=jnp.float32)
        window = window + jnp.dot(from_down_ref[...], down_in_ref[match, step], preferred_element_type=jnp.float32)
        window_ref[...] = window
        made = []
        for pair in range(pairs):
            cr, ci, pf, ps = (
                window_ref[(pair * planes + p) * rows : (pair * planes + p + 1) * rows] for p in range(planes)
            )
            made.append(
                [
                    (cr / 80.0).astype(jnp.bfloat16),
                    (ci / 80.0).astype(jnp.bfloat16),
                    (jnp.sqrt(cr * cr + ci * ci) * lax.rsqrt(pf * ps + epsilon)).astype(jnp.bfloat16),
                ]
            )
        places = [place_of(partners_ref, match, slot, slots) for slot in range(slots)]
        for k in range(3):
            for d in range(slots):
                value = made[0][k]
                for slot in range(1, slots):
                    value = jnp.where(places[slot] == d, made[slot][k], value)
                made_ref[match, d, k, :, columns_of(half, step)] = value
                result_ref[match, step, d, k] = made[slots + d][k]
        result_copy(match, step, half).start()

    steps = 2 * blocks

    def unit_of(t):
        odd = lax.rem(t, 2)
        last = t // (steps - 1)
        first = (steps - t) // steps
        match = (1 - odd) * (1 - first) + odd * last
        step = odd * ((t + 1) // 2) + (1 - odd) * (1 - first) * ((t - 2) // 2) - last
        return match, step

    def body(t, carry):
        compute(*unit_of(t))

        @pl.when(t >= lag)
        def _():
            finish(*unit_of(jnp.maximum(t - lag, 0)))

        return carry

    lax.fori_loop(0, steps, body, 0)

    def rest(t, carry):
        finish(*unit_of(t))
        return carry

    lax.fori_loop(steps - lag, steps, rest, 0)

    def settle(t, carry):
        match = t // blocks
        step = lax.rem(t, blocks)
        got_copy(match, step).wait_send()

        @pl.when(can_up)
        def _():
            up_copy(match, step).wait_send()

        @pl.when(can_down)
        def _():
            down_copy(match, step).wait_send()

        result_copy(match, step, half_of(match)).wait_send()
        result_copy(match, step, 1 - half_of(match)).wait_recv()
        return carry

    lax.fori_loop(0, steps, settle, 0)
    for match in range(2):
        info_copy(match).wait_send()
        halo_copy(match, 1 - half_of(match)).wait_send()


def exchange(partners, shifts, raw):
    slots, _, raw_rows, _ = raw.shape
    groups, strips = lax.axis_size("date"), lax.axis_size("strip")
    half_tiles = raw_rows // 4
    blocks = half_tiles // tiles
    pairs = 2 * slots
    wide = 2 * lanes
    size = tiles * lanes // 4
    ups, downs = pairs * planes * below, pairs * planes * above
    smem = pl.BlockSpec(memory_space=pltpu.SMEM)
    dma = pltpu.SemaphoreType.DMA
    return pl.pallas_call(
        lambda *refs: exchange_kernel(groups, strips, *refs),
        out_shape=jax.ShapeDtypeStruct((2, slots, 3, rows, 2 * blocks * size), jnp.bfloat16),
        in_specs=[smem, smem, pl.BlockSpec(memory_space=pltpu.HBM)],
        out_specs=pl.BlockSpec(memory_space=pltpu.VMEM),
        scratch_shapes=[
            pltpu.VMEM(raw.shape, jnp.bfloat16),
            pltpu.VMEM((slots, 2 * half_tiles + 2, rows, wide), jnp.bfloat16),
            pltpu.VMEM((2, slots, half_tiles + 2, rows, wide), jnp.bfloat16),
            pltpu.VMEM((pairs, tiles, rows, wide), jnp.bfloat16),
            pltpu.VMEM((2, 16, lanes), jnp.float32),
            pltpu.VMEM((2 * pairs, 2, wide, wide), jnp.bfloat16),
            pltpu.VMEM((pairs, 2 * tiles * rows, wide), jnp.float32),
            pltpu.VMEM((2, blocks, pairs * planes * rows, size), jnp.bfloat16),
            pltpu.VMEM((pairs * planes * rows, size), jnp.float32),
            pltpu.VMEM((2, blocks, ups, size), jnp.bfloat16),
            pltpu.VMEM((2, blocks, downs, size), jnp.bfloat16),
            pltpu.VMEM((2, blocks, ups, size), jnp.bfloat16),
            pltpu.VMEM((2, blocks, downs, size), jnp.bfloat16),
            pltpu.VMEM((2, blocks, slots, 3, rows, size), jnp.bfloat16),
            pltpu.VMEM((2, 8, lanes), jnp.int32),
            pltpu.VMEM((2, 8, lanes), jnp.int32),
            pltpu.SMEM((2, 8, lanes), jnp.int32),
            pltpu.VMEM((wide, wide), jnp.bfloat16),
            pltpu.VMEM((wide, wide), jnp.bfloat16),
            pltpu.VMEM((ups + downs, wide), jnp.bfloat16),
            pltpu.VMEM((wide, ups), jnp.bfloat16),
            pltpu.VMEM((wide, downs), jnp.bfloat16),
            dma((2, blocks)),
            dma((2, blocks)),
            dma((2, blocks)),
            dma((2,)),
            dma((2,)),
            dma((2,)),
            dma((2,)),
            dma((2,)),
        ]
        + [dma((2, blocks))] * 6,
        compiler_params=pltpu.CompilerParams(
            vmem_limit_bytes=48 << 20, collective_id=0, has_side_effects=True
        ),
        name="exchange",
    )(partners, shifts, raw)


def hand_out_kernel(made_ref, cross_ref, coherence_ref, sem):
    copies = []
    for match in range(made_ref.shape[0]):
        for d in range(made_ref.shape[1]):
            spot = match * made_ref.shape[1] + d
            copies.append(
                pltpu.make_async_copy(made_ref.at[match, d, 0:2], cross_ref.at[match, d], sem.at[0, spot])
            )
            copies.append(
                pltpu.make_async_copy(made_ref.at[match, d, 2], coherence_ref.at[match, d], sem.at[1, spot])
            )
    for copy in copies:
        copy.start()
    for copy in copies:
        copy.wait()


def hand_out(made):
    matches, dates, _, count, columns = made.shape
    return pl.pallas_call(
        hand_out_kernel,
        out_shape=(
            jax.ShapeDtypeStruct((matches, dates, 2, count, columns), jnp.bfloat16),
            jax.ShapeDtypeStruct((matches, dates, count, columns), jnp.bfloat16),
        ),
        in_specs=[pl.BlockSpec(memory_space=pltpu.VMEM)],
        out_specs=[pl.BlockSpec(memory_space=pltpu.HBM)] * 2,
        scratch_shapes=[pltpu.SemaphoreType.DMA((2, matches * dates))],
        compiler_params=pltpu.CompilerParams(vmem_limit_bytes=4 << 20),
        name="hand_out",
    )(made)


def per_device(acquisitions, partners, band_shifts):
    dates, count, _, samples = acquisitions.shape
    raw = acquisitions.reshape(dates, count, 2, samples // lanes, lanes)
    raw = raw.transpose(0, 1, 3, 2, 4).reshape(dates, count, 2 * (samples // lanes), lanes)
    return hand_out(exchange(partners, band_shifts, raw))


def solution(mesh):
    in_specs = (
        P(("grp", "date"), "strip", None, None),
        P(None, ("grp", "date")),
        P(None, ("grp", "date")),
    )
    out_specs = (
        P(None, ("grp", "date"), None, "strip", None),
        P(None, ("grp", "date"), "strip", None),
    )
    return jax.shard_map(
        per_device, mesh=mesh, in_specs=in_specs, out_specs=out_specs, check_vma=False
    )
```

```python
import math

import jax
import jax.numpy as jnp
from jax import lax
from jax.experimental import pallas as pl
from jax.experimental.pallas import tpu as pltpu
from jax.sharding import PartitionSpec as P

band_width = 0.8
bin_count = 256.0
epsilon = 1e-06
below = 10
above = 9
lanes = 128
rows = 16
tiles = 8
planes = 4
lag = 5
bins = 64
MESH = pl.DeviceIdType.MESH


def make_taps(shifts):
    lane = lax.broadcasted_iota(jnp.int32, shifts.shape, 1)
    inside = (lane < 32) | (lane >= 96)
    positions = jnp.where(lane < 32, lane + 32, lane - 96).astype(jnp.float32)
    centred = positions - 31.5
    hamming = 0.54 - 0.46 * jnp.cos(2.0 * math.pi * positions / 63.0)
    scaled = math.pi * band_width * centred
    lowpass = jnp.where(inside, hamming * band_width * (jnp.sin(scaled) / scaled), 0.0)
    angles = 2.0 * math.pi * shifts.astype(jnp.float32) * centred / bin_count
    return [
        (lowpass * part(angles)).astype(jnp.bfloat16).astype(jnp.float32) for part in (jnp.cos, jnp.sin)
    ]


def circulant(row):
    block = jnp.broadcast_to(row, (32, lanes))
    parts = [pltpu.roll(block, phase, 1, stride=4, stride_axis=0) for phase in range(4)]
    return jnp.concatenate(parts, axis=0).T


def build_weights(taps_ref, weight_ref, spot, source):
    real_part = circulant(taps_ref[0, pl.ds(source, 1), :])
    imag_part = circulant(taps_ref[1, pl.ds(source, 1), :])
    k = lax.broadcasted_iota(jnp.int32, (lanes, lanes), 0)
    c = lax.broadcasted_iota(jnp.int32, (lanes, lanes), 1)
    t = 4 * (c & 31) + (c >> 5)
    inside = jnp.abs(k - t) < 64
    for place, mask in ((0, inside), (1, jnp.logical_not(inside))):
        re = jnp.where(mask, real_part, 0.0)
        im = jnp.where(mask, imag_part, 0.0)
        weight_ref[spot, place, 0:lanes, 0:lanes] = re.astype(jnp.bfloat16)
        weight_ref[spot, place, 0:lanes, lanes:] = im.astype(jnp.bfloat16)
        weight_ref[spot, place, lanes:, 0:lanes] = (-im).astype(jnp.bfloat16)
        weight_ref[spot, place, lanes:, lanes:] = re.astype(jnp.bfloat16)


def partner_slot(pairing, dates):
    return lax.rem(lax.div(pairing, bins), dates)


def shift_of(pairing):
    return lax.rem(pairing, bins) - bins // 2


def place_of(pairing_ref, match, slot, dates):
    place = 0
    for i in range(1, dates):
        place = place + jnp.where(partner_slot(pairing_ref[match, i], dates) == slot, i, 0)
    return place


def iotas(shape):
    return lax.broadcasted_iota(jnp.int32, shape, 0), lax.broadcasted_iota(jnp.int32, shape, 1)


def ones_where(mask):
    return jnp.where(mask, 1.0, 0.0).astype(jnp.bfloat16)


def exchange_kernel(
    groups, strips, pairing_ref, raw_hbm, made_ref,
    raw_ref, own_ref, got_ref, edge_ref, taps_ref, weight_ref, band_ref, looks_ref, window_ref,
    up_out_ref, down_out_ref, up_in_ref, down_in_ref, result_ref,
    info_out_ref, info_in_ref, info_ref, order_ref, near_ref, parts_ref, from_up_ref, from_down_ref,
    raw_sem, got_send, got_recv, halo_send, halo_recv, info_send, info_recv, info_sem,
    up_send, up_recv, down_send, down_recv, result_send, result_recv,
):
    slots = own_ref.shape[0]
    half_tiles = got_ref.shape[2] - 2
    blocks = half_tiles // tiles
    pairs = 2 * slots
    size = tiles * lanes // 4
    ups, downs = up_in_ref.shape[2], down_in_ref.shape[2]
    me = lax.axis_index("date")
    strip = lax.axis_index("strip")
    peer_near = me + 1 - 2 * lax.rem(me, 2)
    peer_far = lax.rem(me + groups // 2, groups)
    half_near = lax.rem(me, 2)
    half_far = me // (groups // 2)
    can_up = strip < strips - 1
    can_down = strip > 0

    def peer_of(match):
        return peer_near * (1 - match) + peer_far * match

    def half_of(match):
        return half_near * (1 - match) + half_far * match

    def block_of(half, step):
        return half * step + (1 - half) * (blocks - 1 - step)

    def raw_copy(half, step):
        spot = pl.ds(pl.multiple_of((half * blocks + block_of(half, step)) * 2 * tiles, 2 * tiles), 2 * tiles)
        return pltpu.make_async_copy(raw_hbm.at[:, :, spot], raw_ref.at[:, :, spot], raw_sem.at[half, step])

    def info_copy(match):
        return pltpu.make_async_remote_copy(
            src_ref=info_out_ref.at[match],
            dst_ref=info_in_ref.at[match],
            send_sem=info_send.at[match],
            recv_sem=info_recv.at[match],
            device_id={"date": peer_of(match)},
            device_id_type=MESH,
        )

    def got_copy(match, step):
        half = 1 - half_of(match)
        spot = block_of(half, step) * tiles + 1
        return pltpu.make_async_remote_copy(
            src_ref=own_ref.at[:, pl.ds(half * half_tiles + spot, tiles)],
            dst_ref=got_ref.at[match, :, pl.ds(spot, tiles)],
            send_sem=got_send.at[match, step],
            recv_sem=got_recv.at[match, step],
            device_id={"date": peer_of(match)},
            device_id_type=MESH,
        )

    def got_wait(match, step):
        spot = block_of(half_of(match), step) * tiles + 1
        return pltpu.make_async_remote_copy(
            src_ref=own_ref.at[:, pl.ds(spot, tiles)],
            dst_ref=got_ref.at[match, :, pl.ds(spot, tiles)],
            send_sem=got_send.at[match, step],
            recv_sem=got_recv.at[match, step],
            device_id={"date": peer_of(match)},
            device_id_type=MESH,
        )

    def halo_copy(match, half):
        return pltpu.make_async_remote_copy(
            src_ref=own_ref.at[:, pl.ds(half_tiles + 1 - half, 1)],
            dst_ref=got_ref.at[match, :, pl.ds((half_tiles + 1) * (1 - half), 1)],
            send_sem=halo_send.at[match],
            recv_sem=halo_recv.at[match],
            device_id={"date": peer_of(match)},
            device_id_type=MESH,
        )

    def up_copy(match, step):
        return pltpu.make_async_remote_copy(
            src_ref=up_out_ref.at[match, step],
            dst_ref=up_in_ref.at[match, step],
            send_sem=up_send.at[match, step],
            recv_sem=up_recv.at[match, step],
            device_id={"strip": strip + 1},
            device_id_type=MESH,
        )

    def down_copy(match, step):
        return pltpu.make_async_remote_copy(
            src_ref=down_out_ref.at[match, step],
            dst_ref=down_in_ref.at[match, step],
            send_sem=down_send.at[match, step],
            recv_sem=down_recv.at[match, step],
            device_id={"strip": strip - 1},
            device_id_type=MESH,
        )

    def columns_of(half, step):
        return pl.ds(pl.multiple_of((half * blocks + block_of(half, step)) * size, size), size)

    def result_copy(match, step, half):
        return pltpu.make_async_remote_copy(
            src_ref=result_ref.at[match, step],
            dst_ref=made_ref.at[match, :, :, :, columns_of(half, step)],
            send_sem=result_send.at[match, step],
            recv_sem=result_recv.at[match, step],
            device_id={"date": peer_of(match)},
            device_id_type=MESH,
        )

    def start_raw(step, carry):
        raw_copy(1 - half_far, step).start()
        raw_copy(half_far, step).start()
        return carry

    lax.fori_loop(0, blocks, start_raw, 0)

    barrier = pltpu.get_barrier_semaphore()
    for peer in (peer_near, peer_far):
        pl.semaphore_signal(barrier, inc=1, device_id={"date": peer}, device_id_type=MESH)

    @pl.when(can_up)
    def _():
        pl.semaphore_signal(barrier, inc=1, device_id={"strip": strip + 1}, device_id_type=MESH)

    @pl.when(can_down)
    def _():
        pl.semaphore_signal(barrier, inc=1, device_id={"strip": strip - 1}, device_id_type=MESH)

    wide = 2 * lanes
    i, j = iotas((wide, wide))
    order_ref[...] = ones_where((i & 15) == (j >> 4)) * ones_where(((i >> 5) == ((j >> 1) & 7)) & (((i >> 4) & 1) == (j & 1)))

    zero_tile = jnp.zeros((slots, 1, rows, wide), jnp.bfloat16)
    own_ref[:, pl.ds(0, 1)] = zero_tile
    own_ref[:, pl.ds(2 * half_tiles + 1, 1)] = zero_tile
    for match in range(2):
        got_ref[match, :, pl.ds((half_tiles + 1) * half_of(match), 1)] = zero_tile

    info_row = lax.broadcasted_iota(jnp.int32, (8, lanes), 0)
    for match in range(2):
        info = jnp.zeros((8, lanes), jnp.int32)
        for d in range(slots):
            info = jnp.where(info_row == d, pairing_ref[match, d], info)
        info_out_ref[match] = info

    def prepare(half, step):
        raw_copy(half, step).wait()
        block = half * blocks + block_of(half, step)
        spot = pl.ds(pl.multiple_of(block * 2 * tiles, 2 * tiles), 2 * tiles)
        images = [raw_ref[d, :, spot].reshape(wide, lanes) for d in range(slots)]
        turned = jnp.dot(
            order_ref[...], jnp.concatenate(images, axis=1), preferred_element_type=jnp.float32
        ).astype(jnp.bfloat16)
        for d in range(slots):
            for q in range(tiles):
                for part in range(2):
                    own_ref[d, block * tiles + 1 + q, :, part * lanes : (part + 1) * lanes] = turned[
                        (2 * q + part) * rows : (2 * q + part + 1) * rows, d * lanes : (d + 1) * lanes
                    ]

    def prepare_both(step):
        prepare(1 - half_far, step)
        prepare(half_far, step)

    def send_both(step):
        got_copy(1, step).start()
        got_copy(0, step).start()

    own_shifts = jnp.zeros((8, lanes), jnp.int32)
    for match in range(2):
        for d in range(slots):
            own_shifts = jnp.where(info_row == match * slots + d, shift_of(pairing_ref[match, d]), own_shifts)
    for part, value in enumerate(make_taps(own_shifts)):
        taps_ref[part, 0:8] = value

    def weigh_own(match):
        def body(slot, carry):
            place = place_of(pairing_ref, match, slot, slots)
            build_weights(taps_ref, weight_ref, match * pairs + slot, match * slots + place)
            return carry

        lax.fori_loop(0, slots, body, 0)

    def weigh_peer(match):
        def body(slot, carry):
            build_weights(taps_ref, weight_ref, match * pairs + slots + slot, 8 + match * slots + slot)
            return carry

        lax.fori_loop(0, slots, body, 0)

    prepare_both(0)
    weigh_own(0)
    pl.semaphore_wait(barrier, 2 + can_up.astype(jnp.int32) + can_down.astype(jnp.int32))
    for match in range(2):
        info_copy(match).start()
        halo_copy(match, 1 - half_of(match)).start()
    send_both(0)
    prepare_both(1)
    send_both(1)

    near_ref[...] = ones_where((i >> 4) == (j >> 4)) * ones_where((j - i <= above) & (i - j <= below))
    i, j = iotas((ups, wide))
    plane = (i * 205) >> 11
    parts_ref[0:ups] = ones_where((plane == (j >> 4)) & ((j & 15) >= i - plane * below + rows - below))
    i, j = iotas((downs, wide))
    plane = (i * 57) >> 9
    parts_ref[ups:] = ones_where((plane == (j >> 4)) & ((j & 15) <= i - plane * above))
    i, j = iotas((wide, ups))
    from_up_ref[...] = ones_where(((i & 15) < below) & (j == (i >> 4) * below + (i & 15)))
    i, j = iotas((wide, downs))
    from_down_ref[...] = ones_where(
        ((i & 15) >= rows - above) & (j == (i >> 4) * above + (i & 15) - (rows - above))
    )

    for match in range(2):
        info_copy(match).wait_recv()
    info_copies = [
        pltpu.make_async_copy(info_in_ref.at[match], info_ref.at[match], info_sem.at[match]) for match in range(2)
    ]
    for copy in info_copies:
        copy.start()
    peer_shifts = jnp.zeros((8, lanes), jnp.int32)
    for match in range(2):
        for d in range(slots):
            peer_shifts = jnp.where(
                info_row == match * slots + d, shift_of(info_in_ref[match, d : d + 1]), peer_shifts
            )
    for part, value in enumerate(make_taps(peer_shifts)):
        taps_ref[part, 8:16] = value
    weigh_peer(0)
    for copy in info_copies:
        copy.wait()

    lane = lax.broadcasted_iota(jnp.int32, (rows, wide), 1) & (lanes - 1)
    from_before = ones_where(lane >= 64)
    from_after = ones_where(lane < 64)

    group = lax.broadcasted_iota(jnp.int32, (rows, lanes), 1) >> 5
    outer = (group == 0) | (group == 3)
    lower = group < 2
    even = (group & 1) == 0

    def pool(v):
        a = jnp.where(outer, v[0], v[2]) + pltpu.roll(jnp.where(outer, v[2], v[0]), 64, 1)
        b = jnp.where(lower, v[1], v[3]) + pltpu.roll(jnp.where(lower, v[3], v[1]), 64, 1)
        return jnp.where(even, a, b) + pltpu.roll(jnp.where(even, b, a), 32, 1)

    def compute(match, step):
        half = half_of(match)
        block = block_of(half, step)
        got_base = block * tiles + 1
        own_base = half * half_tiles + got_base

        @pl.when(step == 0)
        def _():
            halo_copy(match, half).wait_recv()
            got_wait(match, step).wait_recv()

        @pl.when(step < blocks - 1)
        def _():
            got_wait(match, step + 1).wait_recv()

        for d in range(slots):
            for q in range(tiles):
                edge_ref[d, q] = (
                    own_ref[d, own_base + q - 1] * from_before + own_ref[d, own_base + q + 1] * from_after
                )
                edge_ref[slots + d, q] = (
                    got_ref[match, d, got_base + q - 1] * from_before
                    + got_ref[match, d, got_base + q + 1] * from_after
                )

        def own_rows(d):
            return own_ref[d, pl.ds(own_base, tiles)].reshape(tiles * rows, wide)

        def got_rows(d):
            return got_ref[match, d, pl.ds(got_base, tiles)].reshape(tiles * rows, wide)

        def edge_rows(d):
            return edge_ref[d].reshape(tiles * rows, wide)

        for pair in range(pairs):
            if pair < slots:
                place = place_of(pairing_ref, match, pair, slots)
                current = [own_rows(place), got_rows(pair)]
                edges = [edge_rows(place), edge_rows(slots + pair)]
            else:
                place = partner_slot(info_ref[match, pair - slots, 0], slots)
                current = [got_rows(pair - slots), own_rows(place)]
                edges = [edge_rows(pair), edge_rows(place)]
            spot = match * pairs + pair
            out = jnp.dot(
                jnp.concatenate(current, axis=0), weight_ref[spot, 0], preferred_element_type=jnp.float32
            )
            out = out + jnp.dot(
                jnp.concatenate(edges, axis=0), weight_ref[spot, 1], preferred_element_type=jnp.float32
            )
            band_ref[pair] = out
        for pair in range(pairs):
            for a in range(tiles // 4):
                sums = [[], [], [], []]
                for b in range(4):
                    top = (4 * a + b) * rows
                    fr, fi, sr, si = (
                        band_ref[pair, image * tiles * rows + top : image * tiles * rows + top + rows, part * lanes : (part + 1) * lanes]
                        for image in range(2)
                        for part in range(2)
                    )
                    sums[0].append(fr * sr + fi * si)
                    sums[1].append(fi * sr - fr * si)
                    sums[2].append(fr * fr + fi * fi)
                    sums[3].append(sr * sr + si * si)
                for p in range(planes):
                    top = (pair * planes + p) * rows
                    looks_ref[match, step, top : top + rows, a * lanes : (a + 1) * lanes] = pool(sums[p]).astype(
                        jnp.bfloat16
                    )
        parts = jnp.dot(parts_ref[...], looks_ref[match, step], preferred_element_type=jnp.float32)
        parts = parts.astype(jnp.bfloat16)

        @pl.when(can_up)
        def _():
            up_out_ref[match, step] = parts[0:ups]
            up_copy(match, step).start()

        @pl.when(can_down)
        def _():
            down_out_ref[match, step] = parts[ups:]
            down_copy(match, step).start()

    def finish(match, step):
        half = half_of(match)

        @pl.when(can_down)
        def _():
            up_copy(match, step).wait_recv()

        @pl.when(can_up)
        def _():
            down_copy(match, step).wait_recv()

        window = jnp.dot(near_ref[...], looks_ref[match, step], preferred_element_type=jnp.float32)
        window = window + jnp.dot(from_up_ref[...], up_in_ref[match, step], preferred_element_type=jnp.float32)
        window = window + jnp.dot(from_down_ref[...], down_in_ref[match, step], preferred_element_type=jnp.float32)
        window_ref[...] = window
        made = []
        for pair in range(pairs):
            cr, ci, pf, ps = (
                window_ref[(pair * planes + p) * rows : (pair * planes + p + 1) * rows] for p in range(planes)
            )
            made.append(
                [
                    (cr / 80.0).astype(jnp.bfloat16),
                    (ci / 80.0).astype(jnp.bfloat16),
                    (jnp.sqrt(cr * cr + ci * ci) * lax.rsqrt(pf * ps + epsilon)).astype(jnp.bfloat16),
                ]
            )
        places = [place_of(pairing_ref, match, slot, slots) for slot in range(slots)]
        for k in range(3):
            for d in range(slots):
                value = made[0][k]
                for slot in range(1, slots):
                    value = jnp.where(places[slot] == d, made[slot][k], value)
                made_ref[match, d, k, :, columns_of(half, step)] = value
                result_ref[match, step, d, k] = made[slots + d][k]
        result_copy(match, step, half).start()

    steps = 2 * blocks

    @pl.when(jnp.logical_not(can_down))
    def _():
        up_in_ref[...] = jnp.zeros(up_in_ref.shape, up_in_ref.dtype)

    @pl.when(jnp.logical_not(can_up))
    def _():
        down_in_ref[...] = jnp.zeros(down_in_ref.shape, down_in_ref.dtype)

    def reached(t, bound):
        return (t + steps - bound) // steps

    def unit_of(t):
        odd = lax.rem(t, 2)
        early = 1 - reached(t, 3)
        late = reached(t, steps - 4)
        last = reached(t, steps - 1)
        middle = (1 - early) * (1 - late)
        match = middle * odd + late * (1 - last)
        step = early * t + middle * ((t + 2 - odd) // 2 - odd * 2) + late * (1 - last) * (t - blocks + 1)
        return match, step + last * (blocks - 1)

    def body(t, carry):
        @pl.when(t + 2 < blocks)
        def _():
            prepare_both(t + 2)
            send_both(t + 2)

        compute(*unit_of(t))

        @pl.when(t == 0)
        def _():
            weigh_own(1)
            weigh_peer(1)

        @pl.when(t >= lag)
        def _():
            finish(*unit_of(jnp.maximum(t - lag, 0)))

        return carry

    lax.fori_loop(0, steps, body, 0)

    def rest(t, carry):
        finish(*unit_of(t))
        return carry

    lax.fori_loop(steps - lag, steps, rest, 0)

    def settle(t, carry):
        match = t // blocks
        step = lax.rem(t, blocks)
        got_copy(match, step).wait_send()

        @pl.when(can_up)
        def _():
            up_copy(match, step).wait_send()

        @pl.when(can_down)
        def _():
            down_copy(match, step).wait_send()

        result_copy(match, step, half_of(match)).wait_send()
        result_copy(match, step, 1 - half_of(match)).wait_recv()
        return carry

    lax.fori_loop(0, steps, settle, 0)
    for match in range(2):
        info_copy(match).wait_send()
        halo_copy(match, 1 - half_of(match)).wait_send()


def exchange(pairing, raw):
    slots, _, raw_rows, _ = raw.shape
    groups, strips = lax.axis_size("date"), lax.axis_size("strip")
    half_tiles = raw_rows // 4
    blocks = half_tiles // tiles
    pairs = 2 * slots
    wide = 2 * lanes
    size = tiles * lanes // 4
    ups, downs = pairs * planes * below, pairs * planes * above
    dma = pltpu.SemaphoreType.DMA
    return pl.pallas_call(
        lambda *refs: exchange_kernel(groups, strips, *refs),
        out_shape=jax.ShapeDtypeStruct((2, slots, 3, rows, 2 * blocks * size), jnp.bfloat16),
        in_specs=[pl.BlockSpec(memory_space=pltpu.SMEM), pl.BlockSpec(memory_space=pltpu.HBM)],
        out_specs=pl.BlockSpec(memory_space=pltpu.VMEM),
        scratch_shapes=[
            pltpu.VMEM(raw.shape, jnp.bfloat16),
            pltpu.VMEM((slots, 2 * half_tiles + 2, rows, wide), jnp.bfloat16),
            pltpu.VMEM((2, slots, half_tiles + 2, rows, wide), jnp.bfloat16),
            pltpu.VMEM((pairs, tiles, rows, wide), jnp.bfloat16),
            pltpu.VMEM((2, 16, lanes), jnp.float32),
            pltpu.VMEM((2 * pairs, 2, wide, wide), jnp.bfloat16),
            pltpu.VMEM((pairs, 2 * tiles * rows, wide), jnp.float32),
            pltpu.VMEM((2, blocks, pairs * planes * rows, size), jnp.bfloat16),
            pltpu.VMEM((pairs * planes * rows, size), jnp.float32),
            pltpu.VMEM((2, blocks, ups, size), jnp.bfloat16),
            pltpu.VMEM((2, blocks, downs, size), jnp.bfloat16),
            pltpu.VMEM((2, blocks, ups, size), jnp.bfloat16),
            pltpu.VMEM((2, blocks, downs, size), jnp.bfloat16),
            pltpu.VMEM((2, blocks, slots, 3, rows, size), jnp.bfloat16),
            pltpu.VMEM((2, 8, lanes), jnp.int32),
            pltpu.VMEM((2, 8, lanes), jnp.int32),
            pltpu.SMEM((2, 8, lanes), jnp.int32),
            pltpu.VMEM((wide, wide), jnp.bfloat16),
            pltpu.VMEM((wide, wide), jnp.bfloat16),
            pltpu.VMEM((ups + downs, wide), jnp.bfloat16),
            pltpu.VMEM((wide, ups), jnp.bfloat16),
            pltpu.VMEM((wide, downs), jnp.bfloat16),
            dma((2, blocks)),
            dma((2, blocks)),
            dma((2, blocks)),
            dma((2,)),
            dma((2,)),
            dma((2,)),
            dma((2,)),
            dma((2,)),
        ]
        + [dma((2, blocks))] * 6,
        compiler_params=pltpu.CompilerParams(
            vmem_limit_bytes=52000 << 10, collective_id=0, has_side_effects=True
        ),
        name="exchange",
    )(pairing, raw)


def hand_out_kernel(made_ref, cross_ref, coherence_ref, sem):
    copies = []
    for match in range(made_ref.shape[0]):
        for d in range(made_ref.shape[1]):
            spot = match * made_ref.shape[1] + d
            copies.append(
                pltpu.make_async_copy(made_ref.at[match, d, 0:2], cross_ref.at[match, d], sem.at[0, spot])
            )
            copies.append(
                pltpu.make_async_copy(made_ref.at[match, d, 2], coherence_ref.at[match, d], sem.at[1, spot])
            )
    for copy in copies:
        copy.start()
    for copy in copies:
        copy.wait()


def hand_out(made):
    matches, dates, _, count, columns = made.shape
    return pl.pallas_call(
        hand_out_kernel,
        out_shape=(
            jax.ShapeDtypeStruct((matches, dates, 2, count, columns), jnp.bfloat16),
            jax.ShapeDtypeStruct((matches, dates, count, columns), jnp.bfloat16),
        ),
        in_specs=[pl.BlockSpec(memory_space=pltpu.VMEM)],
        out_specs=[pl.BlockSpec(memory_space=pltpu.HBM)] * 2,
        scratch_shapes=[pltpu.SemaphoreType.DMA((2, matches * dates))],
        compiler_params=pltpu.CompilerParams(vmem_limit_bytes=4 << 20),
        name="hand_out",
    )(made)


def per_device(acquisitions, partners, band_shifts):
    dates, count, _, samples = acquisitions.shape
    raw = acquisitions.reshape(dates, count, 2, samples // lanes, lanes)
    raw = raw.transpose(0, 1, 3, 2, 4).reshape(dates, count, 2 * (samples // lanes), lanes)
    return hand_out(exchange(partners * bins + band_shifts + bins // 2, raw))


def solution(mesh):
    in_specs = (
        P(("grp", "date"), "strip", None, None),
        P(None, ("grp", "date")),
        P(None, ("grp", "date")),
    )
    out_specs = (
        P(None, ("grp", "date"), None, "strip", None),
        P(None, ("grp", "date"), "strip", None),
    )
    return jax.shard_map(
        per_device, mesh=mesh, in_specs=in_specs, out_specs=out_specs, check_vma=False
    )
```

```python
import math

import jax
import jax.numpy as jnp
from jax import lax
from jax.experimental import pallas as pl
from jax.experimental.pallas import tpu as pltpu
from jax.sharding import PartitionSpec as P

band_width = 0.8
bin_count = 256.0
epsilon = 1e-06
below = 10
above = 9
lanes = 128
rows = 16
tiles = 8
planes = 4
lag = 5
held = 2
bins = 64
MESH = pl.DeviceIdType.MESH


def make_taps(shifts):
    lane = lax.broadcasted_iota(jnp.int32, shifts.shape, 1)
    inside = (lane < 32) | (lane >= 96)
    positions = jnp.where(lane < 32, lane + 32, lane - 96).astype(jnp.float32)
    centred = positions - 31.5
    hamming = 0.54 - 0.46 * jnp.cos(2.0 * math.pi * positions / 63.0)
    scaled = math.pi * band_width * centred
    lowpass = jnp.where(inside, hamming * band_width * (jnp.sin(scaled) / scaled), 0.0)
    angles = 2.0 * math.pi * shifts.astype(jnp.float32) * centred / bin_count
    return [
        (lowpass * part(angles)).astype(jnp.bfloat16).astype(jnp.float32) for part in (jnp.cos, jnp.sin)
    ]


def circulant(row):
    block = jnp.broadcast_to(row, (32, lanes))
    parts = [pltpu.roll(block, phase, 1, stride=4, stride_axis=0) for phase in range(4)]
    return jnp.concatenate(parts, axis=0).T


def build_weights(taps_ref, weight_ref, spot, source):
    real_part = circulant(taps_ref[0, pl.ds(source, 1), :])
    imag_part = circulant(taps_ref[1, pl.ds(source, 1), :])
    k = lax.broadcasted_iota(jnp.int32, (lanes, lanes), 0)
    c = lax.broadcasted_iota(jnp.int32, (lanes, lanes), 1)
    t = 4 * (c & 31) + (c >> 5)
    inside = jnp.abs(k - t) < 64
    for place, mask in ((0, inside), (1, jnp.logical_not(inside))):
        re = jnp.where(mask, real_part, 0.0)
        im = jnp.where(mask, imag_part, 0.0)
        weight_ref[spot, place, 0:lanes, 0:lanes] = re.astype(jnp.bfloat16)
        weight_ref[spot, place, 0:lanes, lanes:] = im.astype(jnp.bfloat16)
        weight_ref[spot, place, lanes:, 0:lanes] = (-im).astype(jnp.bfloat16)
        weight_ref[spot, place, lanes:, lanes:] = re.astype(jnp.bfloat16)


def partner_slot(pairing, dates):
    return lax.rem(lax.div(pairing, bins), dates)


def shift_of(pairing):
    return lax.rem(pairing, bins) - bins // 2


def place_of(pairing_ref, match, slot, dates):
    place = 0
    for i in range(1, dates):
        place = place + jnp.where(partner_slot(pairing_ref[match, i], dates) == slot, i, 0)
    return place


def iotas(shape):
    return lax.broadcasted_iota(jnp.int32, shape, 0), lax.broadcasted_iota(jnp.int32, shape, 1)


def ones_where(mask):
    return jnp.where(mask, 1.0, 0.0).astype(jnp.bfloat16)


def exchange_kernel(
    groups, strips, pairing_ref, raw_hbm, made_ref,
    raw_ref, own_ref, near_got_ref, far_got_ref, edge_ref, taps_ref, weight_ref, band_ref, looks_ref, window_ref,
    up_out_ref, down_out_ref, up_in_ref, down_in_ref, result_ref,
    info_out_ref, info_in_ref, info_ref, order_ref, inner_ref, parts_ref, from_up_ref, from_down_ref,
    raw_sem, near_send, near_recv, far_send, far_recv, middle_send, middle_recv, info_send, info_recv, info_sem,
    up_send, up_recv, down_send, down_recv, result_send, result_recv,
):
    slots = own_ref.shape[0]
    half_tiles = far_got_ref.shape[1] - 2
    blocks = half_tiles // tiles
    pairs = 2 * slots
    size = tiles * lanes // 4
    ups, downs = up_in_ref.shape[2], down_in_ref.shape[2]
    me = lax.axis_index("date")
    strip = lax.axis_index("strip")
    peer_near = me + 1 - 2 * lax.rem(me, 2)
    peer_far = lax.rem(me + groups // 2, groups)
    half_far = me // (groups // 2)
    can_up = strip < strips - 1
    can_down = strip > 0

    def block_of(half, step):
        return half * step + (1 - half) * (blocks - 1 - step)

    def raw_copy(half, step):
        spot = pl.ds(pl.multiple_of((half * blocks + block_of(half, step)) * 2 * tiles, 2 * tiles), 2 * tiles)
        return pltpu.make_async_copy(raw_hbm.at[:, :, spot], raw_ref.at[:, :, spot], raw_sem.at[half, step])

    def info_copy():
        return pltpu.make_async_remote_copy(
            src_ref=info_out_ref,
            dst_ref=info_in_ref,
            send_sem=info_send,
            recv_sem=info_recv,
            device_id={"date": peer_far},
            device_id_type=MESH,
        )

    def span_of(half, step):
        return block_of(half, step) * tiles + 2 * half

    def near_copy(half, step):
        spot = pl.ds(half * half_tiles + span_of(half, step), tiles)
        return pltpu.make_async_remote_copy(
            src_ref=own_ref.at[:, spot],
            dst_ref=near_got_ref.at[:, spot],
            send_sem=near_send.at[half, step],
            recv_sem=near_recv.at[half, step],
            device_id={"date": peer_near},
            device_id_type=MESH,
        )

    def far_copy(half, step):
        spot = span_of(half, step)
        return pltpu.make_async_remote_copy(
            src_ref=own_ref.at[:, pl.ds(half * half_tiles + spot, tiles)],
            dst_ref=far_got_ref.at[:, pl.ds(spot, tiles)],
            send_sem=far_send.at[step],
            recv_sem=far_recv.at[step],
            device_id={"date": peer_far},
            device_id_type=MESH,
        )

    def middle_near_copy():
        spot = pl.ds(half_tiles, 2)
        return pltpu.make_async_remote_copy(
            src_ref=own_ref.at[:, spot],
            dst_ref=near_got_ref.at[:, spot],
            send_sem=middle_send.at[0],
            recv_sem=middle_recv.at[0],
            device_id={"date": peer_near},
            device_id_type=MESH,
        )

    def middle_far_copy(half):
        return pltpu.make_async_remote_copy(
            src_ref=own_ref.at[:, pl.ds(half_tiles, 2)],
            dst_ref=far_got_ref.at[:, pl.ds(half_tiles * (1 - half), 2)],
            send_sem=middle_send.at[1],
            recv_sem=middle_recv.at[1],
            device_id={"date": peer_far},
            device_id_type=MESH,
        )

    def up_copy(match, step):
        return pltpu.make_async_remote_copy(
            src_ref=up_out_ref.at[match, step],
            dst_ref=up_in_ref.at[match, step],
            send_sem=up_send.at[match, step],
            recv_sem=up_recv.at[match, step],
            device_id={"strip": strip + 1},
            device_id_type=MESH,
        )

    def down_copy(match, step):
        return pltpu.make_async_remote_copy(
            src_ref=down_out_ref.at[match, step],
            dst_ref=down_in_ref.at[match, step],
            send_sem=down_send.at[match, step],
            recv_sem=down_recv.at[match, step],
            device_id={"strip": strip - 1},
            device_id_type=MESH,
        )

    def columns_of(half, step):
        return pl.ds(pl.multiple_of((half * blocks + block_of(half, step)) * size, size), size)

    def result_copy(step, half):
        return pltpu.make_async_remote_copy(
            src_ref=result_ref.at[step],
            dst_ref=made_ref.at[1, :, :, :, columns_of(half, step)],
            send_sem=result_send.at[step],
            recv_sem=result_recv.at[step],
            device_id={"date": peer_far},
            device_id_type=MESH,
        )

    def start_raw(step, carry):
        raw_copy(1 - half_far, step).start()
        raw_copy(half_far, step).start()
        return carry

    lax.fori_loop(0, blocks, start_raw, 0)

    barrier = pltpu.get_barrier_semaphore()
    for peer in (peer_near, peer_far):
        pl.semaphore_signal(barrier, inc=1, device_id={"date": peer}, device_id_type=MESH)

    @pl.when(can_up)
    def _():
        pl.semaphore_signal(barrier, inc=1, device_id={"strip": strip + 1}, device_id_type=MESH)

    @pl.when(can_down)
    def _():
        pl.semaphore_signal(barrier, inc=1, device_id={"strip": strip - 1}, device_id_type=MESH)

    wide = 2 * lanes
    i, j = iotas((wide, wide))
    order_ref[...] = ones_where((i & 15) == (j >> 4)) * ones_where(((i >> 5) == ((j >> 1) & 7)) & (((i >> 4) & 1) == (j & 1)))

    zero_tile = jnp.zeros((slots, 1, rows, wide), jnp.bfloat16)
    own_ref[:, pl.ds(0, 1)] = zero_tile
    own_ref[:, pl.ds(2 * half_tiles + 1, 1)] = zero_tile

    info_row = lax.broadcasted_iota(jnp.int32, (8, lanes), 0)
    info = jnp.zeros((8, lanes), jnp.int32)
    for d in range(slots):
        info = jnp.where(info_row == d, pairing_ref[1, d], info)
    info_out_ref[...] = info

    def prepare(half, step):
        raw_copy(half, step).wait()
        block = half * blocks + block_of(half, step)
        spot = pl.ds(pl.multiple_of(block * 2 * tiles, 2 * tiles), 2 * tiles)
        images = [raw_ref[d, :, spot].reshape(wide, lanes) for d in range(slots)]
        turned = jnp.dot(
            order_ref[...], jnp.concatenate(images, axis=1), preferred_element_type=jnp.float32
        ).astype(jnp.bfloat16)
        for d in range(slots):
            for q in range(tiles):
                for part in range(2):
                    own_ref[d, block * tiles + 1 + q, :, part * lanes : (part + 1) * lanes] = turned[
                        (2 * q + part) * rows : (2 * q + part + 1) * rows, d * lanes : (d + 1) * lanes
                    ]

    def prepare_both(step):
        prepare(1 - half_far, step)
        prepare(half_far, step)

    def send_all(step):
        far_copy(1 - half_far, step).start()
        for half in range(2):
            near_copy(half, step).start()

    own_shifts = jnp.zeros((8, lanes), jnp.int32)
    for match in range(2):
        for d in range(slots):
            own_shifts = jnp.where(info_row == match * slots + d, shift_of(pairing_ref[match, d]), own_shifts)
    for part, value in enumerate(make_taps(own_shifts)):
        taps_ref[part, 0:8] = value

    def weigh_own(match):
        def body(slot, carry):
            place = place_of(pairing_ref, match, slot, slots)
            build_weights(taps_ref, weight_ref, match * slots + slot, match * slots + place)
            return carry

        lax.fori_loop(0, slots, body, 0)

    def weigh_peer():
        def body(slot, carry):
            build_weights(taps_ref, weight_ref, 2 * slots + slot, 8 + slot)
            return carry

        lax.fori_loop(0, slots, body, 0)

    prepare_both(0)
    prepare_both(1)
    pl.semaphore_wait(barrier, 2 + can_up.astype(jnp.int32) + can_down.astype(jnp.int32))
    info_copy().start()
    middle_far_copy(1 - half_far).start()
    middle_near_copy().start()
    send_all(0)
    weigh_own(0)
    prepare_both(2)
    send_all(1)

    i, j = iotas((ups, wide))
    plane = (i * 205) >> 11
    parts_ref[0:ups] = ones_where((plane == (j >> 4)) & ((j & 15) >= i - plane * below + rows - below))
    i, j = iotas((downs, wide))
    plane = (i * 57) >> 9
    parts_ref[ups:] = ones_where((plane == (j >> 4)) & ((j & 15) <= i - plane * above))

    def build_window():
        i, j = iotas((wide, wide))
        inner_ref[...] = ones_where((i >> 4) == (j >> 4)) * ones_where((j - i <= above) & (i - j <= below))
        i, j = iotas((wide, ups))
        from_up_ref[...] = ones_where(((i & 15) < below) & (j == (i >> 4) * below + (i & 15)))
        i, j = iotas((wide, downs))
        from_down_ref[...] = ones_where(
            ((i & 15) >= rows - above) & (j == (i >> 4) * above + (i & 15) - (rows - above))
        )

    def meet_peer():
        weigh_own(1)
        info_copy().wait_recv()
        copy = pltpu.make_async_copy(info_in_ref, info_ref, info_sem)
        copy.start()
        peer_shifts = jnp.zeros((8, lanes), jnp.int32)
        for d in range(slots):
            peer_shifts = jnp.where(info_row == d, shift_of(info_in_ref[d : d + 1]), peer_shifts)
        for part, value in enumerate(make_taps(peer_shifts)):
            taps_ref[part, 8:16] = value
        weigh_peer()
        copy.wait()

    lane = lax.broadcasted_iota(jnp.int32, (rows, wide), 1) & (lanes - 1)
    from_before = ones_where(lane >= 64)
    from_after = ones_where(lane < 64)

    group = lax.broadcasted_iota(jnp.int32, (rows, lanes), 1) >> 5
    outer = (group == 0) | (group == 3)
    lower = group < 2
    even = (group & 1) == 0

    def pool(v):
        a = jnp.where(outer, v[0], v[2]) + pltpu.roll(jnp.where(outer, v[2], v[0]), 64, 1)
        b = jnp.where(lower, v[1], v[3]) + pltpu.roll(jnp.where(lower, v[3], v[1]), 64, 1)
        return jnp.where(even, a, b) + pltpu.roll(jnp.where(even, b, a), 32, 1)

    def make_edges(spot, ref, d, base):
        for q in range(tiles):
            edge_ref[spot, q] = ref[d, base + q - 1] * from_before + ref[d, base + q + 1] * from_after

    def tile_rows(ref, d, base):
        return ref[d, pl.ds(base, tiles)].reshape(tiles * rows, wide)

    def edge_rows(spot):
        return edge_ref[spot].reshape(tiles * rows, wide)

    def combine(pair, current, edges, weight, match, step):
        out = jnp.dot(
            jnp.concatenate(current, axis=0), weight_ref[weight, 0], preferred_element_type=jnp.float32
        )
        out = out + jnp.dot(
            jnp.concatenate(edges, axis=0), weight_ref[weight, 1], preferred_element_type=jnp.float32
        )
        band_ref[pair] = out
        for a in range(tiles // 4):
            sums = [[], [], [], []]
            for b in range(4):
                top = (4 * a + b) * rows
                fr, fi, sr, si = (
                    band_ref[
                        pair,
                        image * tiles * rows + top : image * tiles * rows + top + rows,
                        part * lanes : (part + 1) * lanes,
                    ]
                    for image in range(2)
                    for part in range(2)
                )
                sums[0].append(fr * sr + fi * si)
                sums[1].append(fi * sr - fr * si)
                sums[2].append(fr * fr + fi * fi)
                sums[3].append(sr * sr + si * si)
            for p in range(planes):
                top = (pair * planes + p) * rows
                looks_ref[match, step, top : top + rows, a * lanes : (a + 1) * lanes] = pool(sums[p]).astype(
                    jnp.bfloat16
                )

    def pass_on(match, step):
        parts = jnp.dot(parts_ref[...], looks_ref[match, step], preferred_element_type=jnp.float32)
        parts = parts.astype(jnp.bfloat16)

        @pl.when(can_up)
        def _():
            up_out_ref[match, step] = parts[0:ups]
            up_copy(match, step).start()

        @pl.when(can_down)
        def _():
            down_out_ref[match, step] = parts[ups:]
            down_copy(match, step).start()

    def compute_near(step):
        @pl.when(step == 0)
        def _():
            middle_near_copy().wait_recv()

        for half in range(2):
            near_copy(half, step).wait_recv()
        bases = [half * half_tiles + block_of(half, step) * tiles + 1 for half in range(2)]
        for half in range(2):
            for d in range(slots):
                make_edges(2 * slots * half + d, own_ref, d, bases[half])
                make_edges(2 * slots * half + slots + d, near_got_ref, d, bases[half])
        for half in range(2):
            for slot in range(slots):
                place = place_of(pairing_ref, 0, slot, slots)
                combine(
                    half * slots + slot,
                    [tile_rows(own_ref, place, bases[half]), tile_rows(near_got_ref, slot, bases[half])],
                    [edge_rows(2 * slots * half + place), edge_rows(2 * slots * half + slots + slot)],
                    slot,
                    0,
                    step,
                )

    def compute_far(step):
        @pl.when(step == 0)
        def _():
            middle_far_copy(half_far).wait_recv()

        far_copy(half_far, step).wait_recv()
        got_base = block_of(half_far, step) * tiles + 1
        own_base = half_far * half_tiles + got_base
        for d in range(slots):
            make_edges(d, own_ref, d, own_base)
            make_edges(slots + d, far_got_ref, d, got_base)
        for pair in range(pairs):
            slot = pair % slots
            if pair < slots:
                place = place_of(pairing_ref, 1, slot, slots)
            else:
                place = partner_slot(info_ref[slot, 0], slots)
            current = [tile_rows(own_ref, place, own_base), tile_rows(far_got_ref, slot, got_base)]
            edges = [edge_rows(place), edge_rows(slots + slot)]
            if pair >= slots:
                current, edges = current[::-1], edges[::-1]
            combine(pair, current, edges, slots + pair, 1, step)

    def finish(match, step):
        @pl.when(can_down)
        def _():
            up_copy(match, step).wait_recv()

        @pl.when(can_up)
        def _():
            down_copy(match, step).wait_recv()

        window = jnp.dot(inner_ref[...], looks_ref[match, step], preferred_element_type=jnp.float32)
        window = window + jnp.dot(from_up_ref[...], up_in_ref[match, step], preferred_element_type=jnp.float32)
        window = window + jnp.dot(from_down_ref[...], down_in_ref[match, step], preferred_element_type=jnp.float32)
        window_ref[...] = window
        made = []
        for pair in range(pairs):
            cr, ci, pf, ps = (
                window_ref[(pair * planes + p) * rows : (pair * planes + p + 1) * rows] for p in range(planes)
            )
            made.append(
                [
                    (cr / 80.0).astype(jnp.bfloat16),
                    (ci / 80.0).astype(jnp.bfloat16),
                    (jnp.sqrt(cr * cr + ci * ci) * lax.rsqrt(pf * ps + epsilon)).astype(jnp.bfloat16),
                ]
            )
        places = [place_of(pairing_ref, match, slot, slots) for slot in range(slots)]

        def keep(own, half):
            for k in range(3):
                for d in range(slots):
                    value = own[0][k]
                    for slot in range(1, slots):
                        value = jnp.where(places[slot] == d, own[slot][k], value)
                    made_ref[match, d, k, :, columns_of(half, step)] = value

        @pl.when(match == 0)
        def _():
            for half in range(2):
                keep(made[half * slots : (half + 1) * slots], half)

        @pl.when(match == 1)
        def _():
            for d in range(slots):
                for k in range(3):
                    result_ref[step, d, k] = made[slots + d][k]
            result_copy(step, half_far).start()
            keep(made[:slots], half_far)

    steps = 2 * blocks

    @pl.when(jnp.logical_not(can_down))
    def _():
        up_in_ref[...] = jnp.zeros(up_in_ref.shape, up_in_ref.dtype)

    @pl.when(jnp.logical_not(can_up))
    def _():
        down_in_ref[...] = jnp.zeros(down_in_ref.shape, down_in_ref.dtype)

    def reached(t, bound):
        return (t + steps - bound) // steps

    def unit_of(t):
        odd = lax.rem(t, 2)
        first = 1 - reached(t, 1)
        late = reached(t, steps - 5)
        last = reached(t, steps - 2)
        middle = (1 - first) * (1 - late)
        match = middle * (1 - odd) + late * (1 - last)
        step = middle * ((t + odd) // 2 - (1 - odd)) + late * (1 - last) * (t - blocks + 2) + last * (t - blocks)
        return match, step

    def work_of(t):
        odd = lax.rem(t, 2)
        first = 1 - reached(t, 1)
        last = reached(t, steps - 1)
        match = (1 - odd) * (1 - first) + odd * last
        return match, odd * ((t + 1) // 2) + (1 - odd) * (1 - first) * (t // 2 - 1) - last

    def body(t, carry):
        match, step = work_of(t)

        @pl.when(match == 0)
        def _():
            compute_near(step)

            @pl.when(step < blocks - held)
            def _():
                pass_on(0, step)

        @pl.when(match == 1)
        def _():
            compute_far(step)
            pass_on(1, step)

        @pl.when(t + 3 < blocks)
        def _():
            prepare_both(t + 3)

        @pl.when(t + 2 < blocks)
        def _():
            send_all(t + 2)

        @pl.when(t == 1)
        def _():
            meet_peer()

        @pl.when(t == 2)
        def _():
            build_window()

        @pl.when(t == steps - 1)
        def _():
            for step in range(blocks - held, blocks):
                pass_on(0, step)

        @pl.when(t >= lag)
        def _():
            finish(*unit_of(jnp.maximum(t - lag, 0)))

        return carry

    lax.fori_loop(0, steps, body, 0)

    def rest(t, carry):
        finish(*unit_of(t))
        return carry

    lax.fori_loop(steps - lag, steps, rest, 0)

    def settle(step, carry):
        far_copy(1 - half_far, step).wait_send()
        for half in range(2):
            near_copy(half, step).wait_send()
        for match in range(2):
            @pl.when(can_up)
            def _():
                up_copy(match, step).wait_send()

            @pl.when(can_down)
            def _():
                down_copy(match, step).wait_send()

        result_copy(step, half_far).wait_send()
        result_copy(step, 1 - half_far).wait_recv()
        return carry

    lax.fori_loop(0, blocks, settle, 0)
    info_copy().wait_send()
    middle_far_copy(1 - half_far).wait_send()
    middle_near_copy().wait_send()


def exchange(pairing, raw):
    slots, _, raw_rows, _ = raw.shape
    groups, strips = lax.axis_size("date"), lax.axis_size("strip")
    half_tiles = raw_rows // 4
    blocks = half_tiles // tiles
    pairs = 2 * slots
    wide = 2 * lanes
    size = tiles * lanes // 4
    ups, downs = pairs * planes * below, pairs * planes * above
    dma = pltpu.SemaphoreType.DMA
    return pl.pallas_call(
        lambda *refs: exchange_kernel(groups, strips, *refs),
        out_shape=jax.ShapeDtypeStruct((2, slots, 3, rows, 2 * blocks * size), jnp.bfloat16),
        in_specs=[pl.BlockSpec(memory_space=pltpu.SMEM), pl.BlockSpec(memory_space=pltpu.HBM)],
        out_specs=pl.BlockSpec(memory_space=pltpu.VMEM),
        scratch_shapes=[
            pltpu.VMEM(raw.shape, jnp.bfloat16),
            pltpu.VMEM((slots, 2 * half_tiles + 2, rows, wide), jnp.bfloat16),
            pltpu.VMEM((slots, 2 * half_tiles + 2, rows, wide), jnp.bfloat16),
            pltpu.VMEM((slots, half_tiles + 2, rows, wide), jnp.bfloat16),
            pltpu.VMEM((4 * slots, tiles, rows, wide), jnp.bfloat16),
            pltpu.VMEM((2, 16, lanes), jnp.float32),
            pltpu.VMEM((3 * slots, 2, wide, wide), jnp.bfloat16),
            pltpu.VMEM((pairs, 2 * tiles * rows, wide), jnp.float32),
            pltpu.VMEM((2, blocks, pairs * planes * rows, size), jnp.bfloat16),
            pltpu.VMEM((pairs * planes * rows, size), jnp.float32),
            pltpu.VMEM((2, blocks, ups, size), jnp.bfloat16),
            pltpu.VMEM((2, blocks, downs, size), jnp.bfloat16),
            pltpu.VMEM((2, blocks, ups, size), jnp.bfloat16),
            pltpu.VMEM((2, blocks, downs, size), jnp.bfloat16),
            pltpu.VMEM((blocks, slots, 3, rows, size), jnp.bfloat16),
            pltpu.VMEM((8, lanes), jnp.int32),
            pltpu.VMEM((8, lanes), jnp.int32),
            pltpu.SMEM((8, lanes), jnp.int32),
            pltpu.VMEM((wide, wide), jnp.bfloat16),
            pltpu.VMEM((wide, wide), jnp.bfloat16),
            pltpu.VMEM((ups + downs, wide), jnp.bfloat16),
            pltpu.VMEM((wide, ups), jnp.bfloat16),
            pltpu.VMEM((wide, downs), jnp.bfloat16),
            dma((2, blocks)),
            dma((2, blocks)),
            dma((2, blocks)),
            dma((blocks,)),
            dma((blocks,)),
            dma((2,)),
            dma((2,)),
            dma,
            dma,
            dma,
            dma((2, blocks)),
            dma((2, blocks)),
            dma((2, blocks)),
            dma((2, blocks)),
            dma((blocks,)),
            dma((blocks,)),
        ],
        compiler_params=pltpu.CompilerParams(
            vmem_limit_bytes=52000 << 10, collective_id=0, has_side_effects=True
        ),
        name="exchange",
    )(pairing, raw)


def hand_out_kernel(made_ref, cross_ref, coherence_ref, sem):
    copies = (
        pltpu.make_async_copy(made_ref.at[:, :, 0:2], cross_ref, sem.at[0]),
        pltpu.make_async_copy(made_ref.at[:, :, 2], coherence_ref, sem.at[1]),
    )
    for copy in copies:
        copy.start()
    for copy in copies:
        copy.wait()


def hand_out(made):
    matches, dates, _, count, columns = made.shape
    return pl.pallas_call(
        hand_out_kernel,
        out_shape=(
            jax.ShapeDtypeStruct((matches, dates, 2, count, columns), jnp.bfloat16),
            jax.ShapeDtypeStruct((matches, dates, count, columns), jnp.bfloat16),
        ),
        in_specs=[pl.BlockSpec(memory_space=pltpu.VMEM)],
        out_specs=[pl.BlockSpec(memory_space=pltpu.HBM)] * 2,
        scratch_shapes=[pltpu.SemaphoreType.DMA((2,))],
        compiler_params=pltpu.CompilerParams(vmem_limit_bytes=4 << 20),
        name="hand_out",
    )(made)


def per_device(acquisitions, partners, band_shifts):
    dates, count, _, samples = acquisitions.shape
    raw = acquisitions.reshape(dates, count, 2, samples // lanes, lanes)
    raw = raw.transpose(0, 1, 3, 2, 4).reshape(dates, count, 2 * (samples // lanes), lanes)
    return hand_out(exchange(partners * bins + band_shifts + bins // 2, raw))


def solution(mesh):
    in_specs = (
        P(("grp", "date"), "strip", None, None),
        P(None, ("grp", "date")),
        P(None, ("grp", "date")),
    )
    out_specs = (
        P(None, ("grp", "date"), None, "strip", None),
        P(None, ("grp", "date"), "strip", None),
    )
    return jax.shard_map(
        per_device, mesh=mesh, in_specs=in_specs, out_specs=out_specs, check_vma=False
    )
```

```python
import math

import jax
import jax.numpy as jnp
from jax import lax
from jax.experimental import pallas as pl
from jax.experimental.pallas import tpu as pltpu
from jax.sharding import PartitionSpec as P

band_width = 0.8
bin_count = 256.0
epsilon = 1e-06
below = 10
above = 9
lanes = 128
rows = 16
tiles = 8
planes = 4
lag = 5
held = 2
bins = 64
MESH = pl.DeviceIdType.MESH


def make_taps(shifts):
    lane = lax.broadcasted_iota(jnp.int32, shifts.shape, 1)
    inside = (lane < 32) | (lane >= 96)
    positions = jnp.where(lane < 32, lane + 32, lane - 96).astype(jnp.float32)
    centred = positions - 31.5
    hamming = 0.54 - 0.46 * jnp.cos(2.0 * math.pi * positions / 63.0)
    scaled = math.pi * band_width * centred
    lowpass = jnp.where(inside, hamming * band_width * (jnp.sin(scaled) / scaled), 0.0)
    angles = 2.0 * math.pi * shifts.astype(jnp.float32) * centred / bin_count
    return [
        (lowpass * part(angles)).astype(jnp.bfloat16).astype(jnp.float32) for part in (jnp.cos, jnp.sin)
    ]


def circulant(row):
    block = jnp.broadcast_to(row, (32, lanes))
    parts = [pltpu.roll(block, phase, 1, stride=4, stride_axis=0) for phase in range(4)]
    return jnp.concatenate(parts, axis=0).T


def build_weights(taps_ref, weight_ref, spot, source):
    real_part = circulant(taps_ref[0, pl.ds(source, 1), :])
    imag_part = circulant(taps_ref[1, pl.ds(source, 1), :])
    k = lax.broadcasted_iota(jnp.int32, (lanes, lanes), 0)
    c = lax.broadcasted_iota(jnp.int32, (lanes, lanes), 1)
    t = 4 * (c & 31) + (c >> 5)
    inside = jnp.abs(k - t) < 64
    for place, mask in ((0, inside), (1, jnp.logical_not(inside))):
        re = jnp.where(mask, real_part, 0.0)
        im = jnp.where(mask, imag_part, 0.0)
        weight_ref[spot, place, 0:lanes, 0:lanes] = re.astype(jnp.bfloat16)
        weight_ref[spot, place, 0:lanes, lanes:] = im.astype(jnp.bfloat16)
        weight_ref[spot, place, lanes:, 0:lanes] = (-im).astype(jnp.bfloat16)
        weight_ref[spot, place, lanes:, lanes:] = re.astype(jnp.bfloat16)


def partner_slot(pairing, dates):
    return lax.rem(lax.div(pairing, bins), dates)


def shift_of(pairing):
    return lax.rem(pairing, bins) - bins // 2


def place_of(pairing_ref, match, slot, dates):
    place = 0
    for i in range(1, dates):
        place = place + jnp.where(partner_slot(pairing_ref[match, i], dates) == slot, i, 0)
    return place


def iotas(shape):
    return lax.broadcasted_iota(jnp.int32, shape, 0), lax.broadcasted_iota(jnp.int32, shape, 1)


def ones_where(mask):
    return jnp.where(mask, 1.0, 0.0).astype(jnp.bfloat16)


def exchange_kernel(
    groups, strips, pairing_ref, raw_hbm, made_ref,
    raw_ref, own_ref, near_got_ref, far_got_ref, edge_ref, taps_ref, weight_ref, band_ref, looks_ref, window_ref,
    up_out_ref, down_out_ref, up_in_ref, down_in_ref, result_ref,
    info_out_ref, info_in_ref, info_ref, order_ref, inner_ref, parts_ref, from_up_ref, from_down_ref,
    raw_sem, near_send, near_recv, far_send, far_recv, middle_send, middle_recv, info_send, info_recv, info_sem,
    up_send, up_recv, down_send, down_recv, result_send, result_recv,
):
    slots = own_ref.shape[0]
    half_tiles = far_got_ref.shape[1] - 2
    blocks = half_tiles // tiles
    pairs = 2 * slots
    size = tiles * lanes // 4
    ups, downs = up_in_ref.shape[2], down_in_ref.shape[2]
    me = lax.axis_index("date")
    strip = lax.axis_index("strip")
    peer_near = me + 1 - 2 * lax.rem(me, 2)
    peer_far = lax.rem(me + groups // 2, groups)
    half_far = me // (groups // 2)
    can_up = strip < strips - 1
    can_down = strip > 0

    def block_of(half, step):
        return half * step + (1 - half) * (blocks - 1 - step)

    def raw_copy(half, step):
        spot = pl.ds(pl.multiple_of((half * blocks + block_of(half, step)) * 2 * tiles, 2 * tiles), 2 * tiles)
        return pltpu.make_async_copy(raw_hbm.at[:, :, spot], raw_ref.at[:, :, spot], raw_sem.at[half, step])

    def info_copy():
        return pltpu.make_async_remote_copy(
            src_ref=info_out_ref,
            dst_ref=info_in_ref,
            send_sem=info_send,
            recv_sem=info_recv,
            device_id={"date": peer_far},
            device_id_type=MESH,
        )

    def span_of(half, step):
        return block_of(half, step) * tiles + 2 * half

    def near_copy(half, step):
        spot = pl.ds(half * half_tiles + span_of(half, step), tiles)
        return pltpu.make_async_remote_copy(
            src_ref=own_ref.at[:, spot],
            dst_ref=near_got_ref.at[:, spot],
            send_sem=near_send.at[half, step],
            recv_sem=near_recv.at[half, step],
            device_id={"date": peer_near},
            device_id_type=MESH,
        )

    def far_copy(half, step):
        spot = span_of(half, step)
        return pltpu.make_async_remote_copy(
            src_ref=own_ref.at[:, pl.ds(half * half_tiles + spot, tiles)],
            dst_ref=far_got_ref.at[:, pl.ds(spot, tiles)],
            send_sem=far_send.at[step],
            recv_sem=far_recv.at[step],
            device_id={"date": peer_far},
            device_id_type=MESH,
        )

    def far_last_copy(half):
        spot = span_of(half, blocks - 1) + 1 - half
        return pltpu.make_async_remote_copy(
            src_ref=own_ref.at[:, pl.ds(half * half_tiles + spot, tiles - 1)],
            dst_ref=far_got_ref.at[:, pl.ds(spot, tiles - 1)],
            send_sem=far_send.at[blocks - 1],
            recv_sem=far_recv.at[blocks - 1],
            device_id={"date": peer_far},
            device_id_type=MESH,
        )

    def middle_near_copy():
        spot = pl.ds(half_tiles, 2)
        return pltpu.make_async_remote_copy(
            src_ref=own_ref.at[:, spot],
            dst_ref=near_got_ref.at[:, spot],
            send_sem=middle_send.at[0],
            recv_sem=middle_recv.at[0],
            device_id={"date": peer_near},
            device_id_type=MESH,
        )

    def middle_far_copy(half):
        return pltpu.make_async_remote_copy(
            src_ref=own_ref.at[:, pl.ds(half_tiles, 2)],
            dst_ref=far_got_ref.at[:, pl.ds(half_tiles * (1 - half), 2)],
            send_sem=middle_send.at[1],
            recv_sem=middle_recv.at[1],
            device_id={"date": peer_far},
            device_id_type=MESH,
        )

    def up_copy(match, step):
        return pltpu.make_async_remote_copy(
            src_ref=up_out_ref.at[match, step],
            dst_ref=up_in_ref.at[match, step],
            send_sem=up_send.at[match, step],
            recv_sem=up_recv.at[match, step],
            device_id={"strip": strip + 1},
            device_id_type=MESH,
        )

    def down_copy(match, step):
        return pltpu.make_async_remote_copy(
            src_ref=down_out_ref.at[match, step],
            dst_ref=down_in_ref.at[match, step],
            send_sem=down_send.at[match, step],
            recv_sem=down_recv.at[match, step],
            device_id={"strip": strip - 1},
            device_id_type=MESH,
        )

    def columns_of(half, step):
        return pl.ds(pl.multiple_of((half * blocks + block_of(half, step)) * size, size), size)

    def result_copy(step, half):
        return pltpu.make_async_remote_copy(
            src_ref=result_ref.at[step],
            dst_ref=made_ref.at[1, :, :, :, columns_of(half, step)],
            send_sem=result_send.at[step],
            recv_sem=result_recv.at[step],
            device_id={"date": peer_far},
            device_id_type=MESH,
        )

    def start_raw(step, carry):
        raw_copy(1 - half_far, step).start()
        raw_copy(half_far, step).start()
        return carry

    lax.fori_loop(0, blocks, start_raw, 0)

    barrier = pltpu.get_barrier_semaphore()
    for peer in (peer_near, peer_far):
        pl.semaphore_signal(barrier, inc=1, device_id={"date": peer}, device_id_type=MESH)

    @pl.when(can_up)
    def _():
        pl.semaphore_signal(barrier, inc=1, device_id={"strip": strip + 1}, device_id_type=MESH)

    @pl.when(can_down)
    def _():
        pl.semaphore_signal(barrier, inc=1, device_id={"strip": strip - 1}, device_id_type=MESH)

    wide = 2 * lanes
    i, j = iotas((wide, wide))
    order_ref[...] = ones_where((i & 15) == (j >> 4)) * ones_where(((i >> 5) == ((j >> 1) & 7)) & (((i >> 4) & 1) == (j & 1)))

    zero_tile = jnp.zeros((slots, 1, rows, wide), jnp.bfloat16)
    own_ref[:, pl.ds(0, 1)] = zero_tile
    own_ref[:, pl.ds(2 * half_tiles + 1, 1)] = zero_tile
    far_got_ref[:, pl.ds((half_tiles + 1) * half_far, 1)] = zero_tile

    info_row = lax.broadcasted_iota(jnp.int32, (8, lanes), 0)
    info = jnp.zeros((8, lanes), jnp.int32)
    for d in range(slots):
        info = jnp.where(info_row == d, pairing_ref[1, d], info)
    info_out_ref[...] = info

    def prepare(half, step):
        raw_copy(half, step).wait()
        block = half * blocks + block_of(half, step)
        spot = pl.ds(pl.multiple_of(block * 2 * tiles, 2 * tiles), 2 * tiles)
        images = [raw_ref[d, :, spot].reshape(wide, lanes) for d in range(slots)]
        turned = jnp.dot(
            order_ref[...], jnp.concatenate(images, axis=1), preferred_element_type=jnp.float32
        ).astype(jnp.bfloat16)
        for d in range(slots):
            for q in range(tiles):
                for part in range(2):
                    own_ref[d, block * tiles + 1 + q, :, part * lanes : (part + 1) * lanes] = turned[
                        (2 * q + part) * rows : (2 * q + part + 1) * rows, d * lanes : (d + 1) * lanes
                    ]

    def prepare_both(step):
        prepare(1 - half_far, step)
        prepare(half_far, step)

    def send_all(step):
        step = jnp.int32(step) if isinstance(step, int) else step

        @pl.when(step < blocks - 1)
        def _():
            far_copy(1 - half_far, step).start()

        @pl.when(step == blocks - 1)
        def _():
            far_last_copy(1 - half_far).start()

        for half in range(2):
            near_copy(half, step).start()

    own_shifts = jnp.zeros((8, lanes), jnp.int32)
    for match in range(2):
        for d in range(slots):
            own_shifts = jnp.where(info_row == match * slots + d, shift_of(pairing_ref[match, d]), own_shifts)
    for part, value in enumerate(make_taps(own_shifts)):
        taps_ref[part, 0:8] = value

    def weigh_own(match):
        def body(slot, carry):
            place = place_of(pairing_ref, match, slot, slots)
            build_weights(taps_ref, weight_ref, match * slots + slot, match * slots + place)
            return carry

        lax.fori_loop(0, slots, body, 0)

    def weigh_peer():
        def body(slot, carry):
            build_weights(taps_ref, weight_ref, 2 * slots + slot, 8 + slot)
            return carry

        lax.fori_loop(0, slots, body, 0)

    prepare_both(0)
    pl.semaphore_wait(barrier, 2 + can_up.astype(jnp.int32) + can_down.astype(jnp.int32))
    info_copy().start()
    middle_far_copy(1 - half_far).start()
    middle_near_copy().start()
    prepare_both(1)
    send_all(0)
    weigh_own(0)
    prepare_both(2)
    send_all(1)

    i, j = iotas((ups, wide))
    plane = (i * 205) >> 11
    parts_ref[0:ups] = ones_where((plane == (j >> 4)) & ((j & 15) >= i - plane * below + rows - below))
    i, j = iotas((downs, wide))
    plane = (i * 57) >> 9
    parts_ref[ups:] = ones_where((plane == (j >> 4)) & ((j & 15) <= i - plane * above))

    def build_window():
        i, j = iotas((wide, wide))
        inner_ref[...] = ones_where((i >> 4) == (j >> 4)) * ones_where((j - i <= above) & (i - j <= below))
        i, j = iotas((wide, ups))
        from_up_ref[...] = ones_where(((i & 15) < below) & (j == (i >> 4) * below + (i & 15)))
        i, j = iotas((wide, downs))
        from_down_ref[...] = ones_where(
            ((i & 15) >= rows - above) & (j == (i >> 4) * above + (i & 15) - (rows - above))
        )

    def meet_peer():
        weigh_own(1)
        info_copy().wait_recv()
        copy = pltpu.make_async_copy(info_in_ref, info_ref, info_sem)
        copy.start()
        peer_shifts = jnp.zeros((8, lanes), jnp.int32)
        for d in range(slots):
            peer_shifts = jnp.where(info_row == d, shift_of(info_in_ref[d : d + 1]), peer_shifts)
        for part, value in enumerate(make_taps(peer_shifts)):
            taps_ref[part, 8:16] = value
        weigh_peer()
        copy.wait()

    lane = lax.broadcasted_iota(jnp.int32, (rows, wide), 1) & (lanes - 1)
    from_before = ones_where(lane >= 64)
    from_after = ones_where(lane < 64)

    group = lax.broadcasted_iota(jnp.int32, (rows, lanes), 1) >> 5
    outer = (group == 0) | (group == 3)
    lower = group < 2
    even = (group & 1) == 0

    def pool(v):
        a = jnp.where(outer, v[0], v[2]) + pltpu.roll(jnp.where(outer, v[2], v[0]), 64, 1)
        b = jnp.where(lower, v[1], v[3]) + pltpu.roll(jnp.where(lower, v[3], v[1]), 64, 1)
        return jnp.where(even, a, b) + pltpu.roll(jnp.where(even, b, a), 32, 1)

    def make_edges(spot, ref, d, base):
        for q in range(tiles):
            edge_ref[spot, q] = ref[d, base + q - 1] * from_before + ref[d, base + q + 1] * from_after

    def tile_rows(ref, d, base):
        return ref[d, pl.ds(base, tiles)].reshape(tiles * rows, wide)

    def edge_rows(spot):
        return edge_ref[spot].reshape(tiles * rows, wide)

    def combine(pair, current, edges, weight, match, step):
        out = jnp.dot(
            jnp.concatenate(current, axis=0), weight_ref[weight, 0], preferred_element_type=jnp.float32
        )
        out = out + jnp.dot(
            jnp.concatenate(edges, axis=0), weight_ref[weight, 1], preferred_element_type=jnp.float32
        )
        band_ref[pair] = out
        for a in range(tiles // 4):
            sums = [[], [], [], []]
            for b in range(4):
                top = (4 * a + b) * rows
                fr, fi, sr, si = (
                    band_ref[
                        pair,
                        image * tiles * rows + top : image * tiles * rows + top + rows,
                        part * lanes : (part + 1) * lanes,
                    ]
                    for image in range(2)
                    for part in range(2)
                )
                sums[0].append(fr * sr + fi * si)
                sums[1].append(fi * sr - fr * si)
                sums[2].append(fr * fr + fi * fi)
                sums[3].append(sr * sr + si * si)
            for p in range(planes):
                top = (pair * planes + p) * rows
                looks_ref[match, step, top : top + rows, a * lanes : (a + 1) * lanes] = pool(sums[p]).astype(
                    jnp.bfloat16
                )

    def pass_on(match, step):
        parts = jnp.dot(parts_ref[...], looks_ref[match, step], preferred_element_type=jnp.float32)
        parts = parts.astype(jnp.bfloat16)

        @pl.when(can_up)
        def _():
            up_out_ref[match, step] = parts[0:ups]
            up_copy(match, step).start()

        @pl.when(can_down)
        def _():
            down_out_ref[match, step] = parts[ups:]
            down_copy(match, step).start()

    def compute_near(step):
        @pl.when(step == 0)
        def _():
            middle_near_copy().wait_recv()

        for half in range(2):
            near_copy(half, step).wait_recv()
        bases = [half * half_tiles + block_of(half, step) * tiles + 1 for half in range(2)]
        for half in range(2):
            for d in range(slots):
                make_edges(2 * slots * half + d, own_ref, d, bases[half])
                make_edges(2 * slots * half + slots + d, near_got_ref, d, bases[half])
        for half in range(2):
            for slot in range(slots):
                place = place_of(pairing_ref, 0, slot, slots)
                combine(
                    half * slots + slot,
                    [tile_rows(own_ref, place, bases[half]), tile_rows(near_got_ref, slot, bases[half])],
                    [edge_rows(2 * slots * half + place), edge_rows(2 * slots * half + slots + slot)],
                    slot,
                    0,
                    step,
                )

    def compute_far(step):
        @pl.when(step == 0)
        def _():
            middle_far_copy(half_far).wait_recv()

        @pl.when(step < blocks - 1)
        def _():
            far_copy(half_far, step).wait_recv()

        @pl.when(step == blocks - 1)
        def _():
            far_last_copy(half_far).wait_recv()

        got_base = block_of(half_far, step) * tiles + 1
        own_base = half_far * half_tiles + got_base
        for d in range(slots):
            make_edges(d, own_ref, d, own_base)
            make_edges(slots + d, far_got_ref, d, got_base)
        for pair in range(pairs):
            slot = pair % slots
            if pair < slots:
                place = place_of(pairing_ref, 1, slot, slots)
            else:
                place = partner_slot(info_ref[slot, 0], slots)
            current = [tile_rows(own_ref, place, own_base), tile_rows(far_got_ref, slot, got_base)]
            edges = [edge_rows(place), edge_rows(slots + slot)]
            if pair >= slots:
                current, edges = current[::-1], edges[::-1]
            combine(pair, current, edges, slots + pair, 1, step)

    def finish(match, step):
        @pl.when(can_down)
        def _():
            up_copy(match, step).wait_recv()

        @pl.when(can_up)
        def _():
            down_copy(match, step).wait_recv()

        window = jnp.dot(inner_ref[...], looks_ref[match, step], preferred_element_type=jnp.float32)
        window = window + jnp.dot(from_up_ref[...], up_in_ref[match, step], preferred_element_type=jnp.float32)
        window = window + jnp.dot(from_down_ref[...], down_in_ref[match, step], preferred_element_type=jnp.float32)
        window_ref[...] = window
        made = []
        for pair in range(pairs):
            cr, ci, pf, ps = (
                window_ref[(pair * planes + p) * rows : (pair * planes + p + 1) * rows] for p in range(planes)
            )
            made.append(
                [
                    (cr * (1.0 / 80.0)).astype(jnp.bfloat16),
                    (ci * (1.0 / 80.0)).astype(jnp.bfloat16),
                    (jnp.sqrt(cr * cr + ci * ci) * lax.rsqrt(pf * ps + epsilon)).astype(jnp.bfloat16),
                ]
            )
        places = [place_of(pairing_ref, match, slot, slots) for slot in range(slots)]

        def keep(own, half):
            for k in range(3):
                for d in range(slots):
                    value = own[0][k]
                    for slot in range(1, slots):
                        value = jnp.where(places[slot] == d, own[slot][k], value)
                    made_ref[match, d, k, :, columns_of(half, step)] = value

        @pl.when(match == 0)
        def _():
            for half in range(2):
                keep(made[half * slots : (half + 1) * slots], half)

        @pl.when(match == 1)
        def _():
            for d in range(slots):
                for k in range(3):
                    result_ref[step, d, k] = made[slots + d][k]
            result_copy(step, half_far).start()
            keep(made[:slots], half_far)

    steps = 2 * blocks

    @pl.when(jnp.logical_not(can_down))
    def _():
        up_in_ref[...] = jnp.zeros(up_in_ref.shape, up_in_ref.dtype)

    @pl.when(jnp.logical_not(can_up))
    def _():
        down_in_ref[...] = jnp.zeros(down_in_ref.shape, down_in_ref.dtype)

    def reached(t, bound):
        return (t + steps - bound) // steps

    def unit_of(t):
        odd = lax.rem(t, 2)
        first = 1 - reached(t, 1)
        late = reached(t, steps - 5)
        last = reached(t, steps - 2)
        middle = (1 - first) * (1 - late)
        match = middle * (1 - odd) + late * (1 - last)
        step = middle * ((t + odd) // 2 - (1 - odd)) + late * (1 - last) * (t - blocks + 2) + last * (t - blocks)
        return match, step

    def work_of(t):
        odd = lax.rem(t, 2)
        first = 1 - reached(t, 1)
        last = reached(t, steps - 1)
        match = (1 - odd) * (1 - first) + odd * last
        return match, odd * ((t + 1) // 2) + (1 - odd) * (1 - first) * (t // 2 - 1) - last

    def body(t, carry):
        match, step = work_of(t)

        @pl.when(match == 0)
        def _():
            compute_near(step)

            @pl.when(step < blocks - held)
            def _():
                pass_on(0, step)

        @pl.when(match == 1)
        def _():
            compute_far(step)
            pass_on(1, step)

        @pl.when(t + 3 < blocks)
        def _():
            prepare_both(t + 3)

        @pl.when(t + 2 < blocks)
        def _():
            send_all(t + 2)

        @pl.when(t == 1)
        def _():
            meet_peer()

        @pl.when(t == 2)
        def _():
            build_window()

        @pl.when(t == steps - 1)
        def _():
            for step in range(blocks - held, blocks):
                pass_on(0, step)

        @pl.when(t >= lag)
        def _():
            finish(*unit_of(jnp.maximum(t - lag, 0)))

        return carry

    lax.fori_loop(0, steps, body, 0)

    def rest(t, carry):
        finish(*unit_of(t))
        return carry

    lax.fori_loop(steps - lag, steps, rest, 0)

    def settle(step, carry):
        @pl.when(step < blocks - 1)
        def _():
            far_copy(1 - half_far, step).wait_send()

        @pl.when(step == blocks - 1)
        def _():
            far_last_copy(1 - half_far).wait_send()

        for half in range(2):
            near_copy(half, step).wait_send()
        for match in range(2):
            @pl.when(can_up)
            def _():
                up_copy(match, step).wait_send()

            @pl.when(can_down)
            def _():
                down_copy(match, step).wait_send()

        result_copy(step, half_far).wait_send()
        result_copy(step, 1 - half_far).wait_recv()
        return carry

    lax.fori_loop(0, blocks, settle, 0)
    info_copy().wait_send()
    middle_far_copy(1 - half_far).wait_send()
    middle_near_copy().wait_send()


def exchange(pairing, raw):
    slots, _, raw_rows, _ = raw.shape
    groups, strips = lax.axis_size("date"), lax.axis_size("strip")
    half_tiles = raw_rows // 4
    blocks = half_tiles // tiles
    pairs = 2 * slots
    wide = 2 * lanes
    size = tiles * lanes // 4
    ups, downs = pairs * planes * below, pairs * planes * above
    dma = pltpu.SemaphoreType.DMA
    return pl.pallas_call(
        lambda *refs: exchange_kernel(groups, strips, *refs),
        out_shape=jax.ShapeDtypeStruct((2, slots, 3, rows, 2 * blocks * size), jnp.bfloat16),
        in_specs=[pl.BlockSpec(memory_space=pltpu.SMEM), pl.BlockSpec(memory_space=pltpu.HBM)],
        out_specs=pl.BlockSpec(memory_space=pltpu.VMEM),
        scratch_shapes=[
            pltpu.VMEM(raw.shape, jnp.bfloat16),
            pltpu.VMEM((slots, 2 * half_tiles + 2, rows, wide), jnp.bfloat16),
            pltpu.VMEM((slots, 2 * half_tiles + 2, rows, wide), jnp.bfloat16),
            pltpu.VMEM((slots, half_tiles + 2, rows, wide), jnp.bfloat16),
            pltpu.VMEM((4 * slots, tiles, rows, wide), jnp.bfloat16),
            pltpu.VMEM((2, 16, lanes), jnp.float32),
            pltpu.VMEM((3 * slots, 2, wide, wide), jnp.bfloat16),
            pltpu.VMEM((pairs, 2 * tiles * rows, wide), jnp.float32),
            pltpu.VMEM((2, blocks, pairs * planes * rows, size), jnp.bfloat16),
            pltpu.VMEM((pairs * planes * rows, size), jnp.float32),
            pltpu.VMEM((2, blocks, ups, size), jnp.bfloat16),
            pltpu.VMEM((2, blocks, downs, size), jnp.bfloat16),
            pltpu.VMEM((2, blocks, ups, size), jnp.bfloat16),
            pltpu.VMEM((2, blocks, downs, size), jnp.bfloat16),
            pltpu.VMEM((blocks, slots, 3, rows, size), jnp.bfloat16),
            pltpu.VMEM((8, lanes), jnp.int32),
            pltpu.VMEM((8, lanes), jnp.int32),
            pltpu.SMEM((8, lanes), jnp.int32),
            pltpu.VMEM((wide, wide), jnp.bfloat16),
            pltpu.VMEM((wide, wide), jnp.bfloat16),
            pltpu.VMEM((ups + downs, wide), jnp.bfloat16),
            pltpu.VMEM((wide, ups), jnp.bfloat16),
            pltpu.VMEM((wide, downs), jnp.bfloat16),
            dma((2, blocks)),
            dma((2, blocks)),
            dma((2, blocks)),
            dma((blocks,)),
            dma((blocks,)),
            dma((2,)),
            dma((2,)),
            dma,
            dma,
            dma,
            dma((2, blocks)),
            dma((2, blocks)),
            dma((2, blocks)),
            dma((2, blocks)),
            dma((blocks,)),
            dma((blocks,)),
        ],
        compiler_params=pltpu.CompilerParams(
            vmem_limit_bytes=52000 << 10, collective_id=0, has_side_effects=True
        ),
        name="exchange",
    )(pairing, raw)


def hand_out_kernel(made_ref, cross_ref, coherence_ref, sem):
    copies = (
        pltpu.make_async_copy(made_ref.at[:, :, 0:2], cross_ref, sem.at[0]),
        pltpu.make_async_copy(made_ref.at[:, :, 2], coherence_ref, sem.at[1]),
    )
    for copy in copies:
        copy.start()
    for copy in copies:
        copy.wait()


def hand_out(made):
    matches, dates, _, count, columns = made.shape
    return pl.pallas_call(
        hand_out_kernel,
        out_shape=(
            jax.ShapeDtypeStruct((matches, dates, 2, count, columns), jnp.bfloat16),
            jax.ShapeDtypeStruct((matches, dates, count, columns), jnp.bfloat16),
        ),
        in_specs=[pl.BlockSpec(memory_space=pltpu.VMEM)],
        out_specs=[pl.BlockSpec(memory_space=pltpu.HBM)] * 2,
        scratch_shapes=[pltpu.SemaphoreType.DMA((2,))],
        compiler_params=pltpu.CompilerParams(vmem_limit_bytes=4 << 20),
        name="hand_out",
    )(made)


def per_device(acquisitions, partners, band_shifts):
    dates, count, _, samples = acquisitions.shape
    raw = acquisitions.reshape(dates, count, 2, samples // lanes, lanes)
    raw = raw.transpose(0, 1, 3, 2, 4).reshape(dates, count, 2 * (samples // lanes), lanes)
    return hand_out(exchange(partners * bins + band_shifts + bins // 2, raw))


def solution(mesh):
    in_specs = (
        P(("grp", "date"), "strip", None, None),
        P(None, ("grp", "date")),
        P(None, ("grp", "date")),
    )
    out_specs = (
        P(None, ("grp", "date"), None, "strip", None),
        P(None, ("grp", "date"), "strip", None),
    )
    return jax.shard_map(
        per_device, mesh=mesh, in_specs=in_specs, out_specs=out_specs, check_vma=False
    )
```

```python
import math

import jax
import jax.numpy as jnp
from jax import lax
from jax.experimental import pallas as pl
from jax.experimental.pallas import tpu as pltpu
from jax.sharding import PartitionSpec as P

band_width = 0.8
bin_count = 256.0
epsilon = 1e-06
below = 10
above = 9
lanes = 128
rows = 16
tiles = 8
planes = 4
lag = 6
held = 2
bins = 64
MESH = pl.DeviceIdType.MESH


def make_taps(shifts):
    lane = lax.broadcasted_iota(jnp.int32, shifts.shape, 1)
    inside = (lane < 32) | (lane >= 96)
    positions = jnp.where(lane < 32, lane + 32, lane - 96).astype(jnp.float32)
    centred = positions - 31.5
    hamming = 0.54 - 0.46 * jnp.cos(2.0 * math.pi * positions / 63.0)
    scaled = math.pi * band_width * centred
    lowpass = jnp.where(inside, hamming * band_width * (jnp.sin(scaled) / scaled), 0.0)
    angles = 2.0 * math.pi * shifts.astype(jnp.float32) * centred / bin_count
    return [
        (lowpass * part(angles)).astype(jnp.bfloat16).astype(jnp.float32) for part in (jnp.cos, jnp.sin)
    ]


def circulant(row):
    block = jnp.broadcast_to(row, (32, lanes))
    parts = [pltpu.roll(block, phase, 1, stride=4, stride_axis=0) for phase in range(4)]
    return jnp.concatenate(parts, axis=0).T


def build_weights(taps_ref, weight_ref, spot, source):
    real_part = circulant(taps_ref[0, pl.ds(source, 1), :])
    imag_part = circulant(taps_ref[1, pl.ds(source, 1), :])
    k = lax.broadcasted_iota(jnp.int32, (lanes, lanes), 0)
    c = lax.broadcasted_iota(jnp.int32, (lanes, lanes), 1)
    t = 4 * (c & 31) + (c >> 5)
    inside = jnp.abs(k - t) < 64
    for place, mask in ((0, inside), (1, jnp.logical_not(inside))):
        re = jnp.where(mask, real_part, 0.0)
        im = jnp.where(mask, imag_part, 0.0)
        weight_ref[spot, place, 0:lanes, 0:lanes] = re.astype(jnp.bfloat16)
        weight_ref[spot, place, 0:lanes, lanes:] = im.astype(jnp.bfloat16)
        weight_ref[spot, place, lanes:, 0:lanes] = (-im).astype(jnp.bfloat16)
        weight_ref[spot, place, lanes:, lanes:] = re.astype(jnp.bfloat16)


def partner_slot(pairing, dates):
    return lax.rem(lax.div(pairing, bins), dates)


def shift_of(pairing):
    return lax.rem(pairing, bins) - bins // 2


def place_of(pairing_ref, match, slot, dates):
    place = 0
    for i in range(1, dates):
        place = place + jnp.where(partner_slot(pairing_ref[match, i], dates) == slot, i, 0)
    return place


def iotas(shape):
    return lax.broadcasted_iota(jnp.int32, shape, 0), lax.broadcasted_iota(jnp.int32, shape, 1)


def ones_where(mask):
    return jnp.where(mask, 1.0, 0.0).astype(jnp.bfloat16)


def exchange_kernel(
    groups, strips, pairing_ref, raw_hbm, made_ref,
    raw_ref, own_ref, near_got_ref, far_got_ref, edge_ref, taps_ref, weight_ref, band_ref, looks_ref, window_ref,
    up_out_ref, down_out_ref, up_in_ref, down_in_ref, result_ref,
    info_out_ref, info_in_ref, info_ref, order_ref, inner_ref, parts_ref, from_up_ref, from_down_ref,
    raw_sem, near_send, near_recv, far_send, far_recv, middle_send, middle_recv, info_send, info_recv, info_sem,
    up_send, up_recv, down_send, down_recv, result_send, result_recv,
):
    slots = own_ref.shape[0]
    half_tiles = far_got_ref.shape[1] - 2
    blocks = half_tiles // tiles
    pairs = 2 * slots
    size = tiles * lanes // 4
    ups, downs = up_in_ref.shape[2], down_in_ref.shape[2]
    me = lax.axis_index("date")
    strip = lax.axis_index("strip")
    peer_near = me + 1 - 2 * lax.rem(me, 2)
    peer_far = lax.rem(me + groups // 2, groups)
    half_far = me // (groups // 2)
    can_up = strip < strips - 1
    can_down = strip > 0

    def block_of(half, step):
        return half * step + (1 - half) * (blocks - 1 - step)

    def raw_copy(half, step):
        spot = pl.ds(pl.multiple_of((half * blocks + block_of(half, step)) * 2 * tiles, 2 * tiles), 2 * tiles)
        return pltpu.make_async_copy(raw_hbm.at[:, :, spot], raw_ref.at[:, :, spot], raw_sem.at[half, step])

    def info_copy():
        return pltpu.make_async_remote_copy(
            src_ref=info_out_ref,
            dst_ref=info_in_ref,
            send_sem=info_send,
            recv_sem=info_recv,
            device_id={"date": peer_far},
            device_id_type=MESH,
        )

    def span_of(half, step):
        return block_of(half, step) * tiles + 2 * half

    def near_copy(half, step):
        spot = pl.ds(half * half_tiles + span_of(half, step), tiles)
        return pltpu.make_async_remote_copy(
            src_ref=own_ref.at[:, spot],
            dst_ref=near_got_ref.at[:, spot],
            send_sem=near_send.at[half, step],
            recv_sem=near_recv.at[half, step],
            device_id={"date": peer_near},
            device_id_type=MESH,
        )

    def far_copy(half, step):
        spot = span_of(half, step)
        return pltpu.make_async_remote_copy(
            src_ref=own_ref.at[:, pl.ds(half * half_tiles + spot, tiles)],
            dst_ref=far_got_ref.at[:, pl.ds(spot, tiles)],
            send_sem=far_send.at[step],
            recv_sem=far_recv.at[step],
            device_id={"date": peer_far},
            device_id_type=MESH,
        )

    def far_last_copy(half):
        spot = span_of(half, blocks - 1) + 1 - half
        return pltpu.make_async_remote_copy(
            src_ref=own_ref.at[:, pl.ds(half * half_tiles + spot, tiles - 1)],
            dst_ref=far_got_ref.at[:, pl.ds(spot, tiles - 1)],
            send_sem=far_send.at[blocks - 1],
            recv_sem=far_recv.at[blocks - 1],
            device_id={"date": peer_far},
            device_id_type=MESH,
        )

    def middle_near_copy():
        spot = pl.ds(half_tiles, 2)
        return pltpu.make_async_remote_copy(
            src_ref=own_ref.at[:, spot],
            dst_ref=near_got_ref.at[:, spot],
            send_sem=middle_send.at[0],
            recv_sem=middle_recv.at[0],
            device_id={"date": peer_near},
            device_id_type=MESH,
        )

    def middle_far_copy(half):
        return pltpu.make_async_remote_copy(
            src_ref=own_ref.at[:, pl.ds(half_tiles, 2)],
            dst_ref=far_got_ref.at[:, pl.ds(half_tiles * (1 - half), 2)],
            send_sem=middle_send.at[1],
            recv_sem=middle_recv.at[1],
            device_id={"date": peer_far},
            device_id_type=MESH,
        )

    def up_copy(match, step):
        return pltpu.make_async_remote_copy(
            src_ref=up_out_ref.at[match, step],
            dst_ref=up_in_ref.at[match, step],
            send_sem=up_send.at[match, step],
            recv_sem=up_recv.at[match, step],
            device_id={"strip": strip + 1},
            device_id_type=MESH,
        )

    def down_copy(match, step):
        return pltpu.make_async_remote_copy(
            src_ref=down_out_ref.at[match, step],
            dst_ref=down_in_ref.at[match, step],
            send_sem=down_send.at[match, step],
            recv_sem=down_recv.at[match, step],
            device_id={"strip": strip - 1},
            device_id_type=MESH,
        )

    def columns_of(half, step):
        return pl.ds(pl.multiple_of((half * blocks + block_of(half, step)) * size, size), size)

    def result_copy(step, half):
        return pltpu.make_async_remote_copy(
            src_ref=result_ref.at[step],
            dst_ref=made_ref.at[1, :, :, :, columns_of(half, step)],
            send_sem=result_send.at[step],
            recv_sem=result_recv.at[step],
            device_id={"date": peer_far},
            device_id_type=MESH,
        )

    def start_raw(step, carry):
        raw_copy(1 - half_far, step).start()
        raw_copy(half_far, step).start()
        return carry

    lax.fori_loop(0, blocks, start_raw, 0)

    barrier = pltpu.get_barrier_semaphore()
    for peer in (peer_near, peer_far):
        pl.semaphore_signal(barrier, inc=1, device_id={"date": peer}, device_id_type=MESH)

    @pl.when(can_up)
    def _():
        pl.semaphore_signal(barrier, inc=1, device_id={"strip": strip + 1}, device_id_type=MESH)

    @pl.when(can_down)
    def _():
        pl.semaphore_signal(barrier, inc=1, device_id={"strip": strip - 1}, device_id_type=MESH)

    wide = 2 * lanes
    i, j = iotas((wide, wide))
    order_ref[...] = ones_where((i & 15) == (j >> 4)) * ones_where(((i >> 5) == ((j >> 1) & 7)) & (((i >> 4) & 1) == (j & 1)))

    zero_tile = jnp.zeros((slots, 1, rows, wide), jnp.bfloat16)
    own_ref[:, pl.ds(0, 1)] = zero_tile
    own_ref[:, pl.ds(2 * half_tiles + 1, 1)] = zero_tile
    far_got_ref[:, pl.ds((half_tiles + 1) * half_far, 1)] = zero_tile

    info_row = lax.broadcasted_iota(jnp.int32, (8, lanes), 0)
    info = jnp.zeros((8, lanes), jnp.int32)
    for d in range(slots):
        info = jnp.where(info_row == d, pairing_ref[1, d], info)
    info_out_ref[...] = info

    def prepare(half, step):
        raw_copy(half, step).wait()
        block = half * blocks + block_of(half, step)
        spot = pl.ds(pl.multiple_of(block * 2 * tiles, 2 * tiles), 2 * tiles)
        images = [raw_ref[d, :, spot].reshape(wide, lanes) for d in range(slots)]
        turned = jnp.dot(
            order_ref[...], jnp.concatenate(images, axis=1), preferred_element_type=jnp.float32
        ).astype(jnp.bfloat16)
        for d in range(slots):
            for q in range(tiles):
                for part in range(2):
                    own_ref[d, block * tiles + 1 + q, :, part * lanes : (part + 1) * lanes] = turned[
                        (2 * q + part) * rows : (2 * q + part + 1) * rows, d * lanes : (d + 1) * lanes
                    ]

    def prepare_both(step):
        prepare(1 - half_far, step)
        prepare(half_far, step)

    def send_all(step):
        step = jnp.int32(step) if isinstance(step, int) else step

        @pl.when(step < blocks - 1)
        def _():
            far_copy(1 - half_far, step).start()

        @pl.when(step == blocks - 1)
        def _():
            far_last_copy(1 - half_far).start()

        for half in range(2):
            near_copy(half, step).start()

    own_shifts = jnp.zeros((8, lanes), jnp.int32)
    for match in range(2):
        for d in range(slots):
            own_shifts = jnp.where(info_row == match * slots + d, shift_of(pairing_ref[match, d]), own_shifts)
    for part, value in enumerate(make_taps(own_shifts)):
        taps_ref[part, 0:8] = value

    def weigh_own(match):
        def body(slot, carry):
            place = place_of(pairing_ref, match, slot, slots)
            build_weights(taps_ref, weight_ref, match * slots + slot, match * slots + place)
            return carry

        lax.fori_loop(0, slots, body, 0)

    def weigh_peer():
        def body(slot, carry):
            build_weights(taps_ref, weight_ref, 2 * slots + slot, 8 + slot)
            return carry

        lax.fori_loop(0, slots, body, 0)

    prepare_both(0)
    pl.semaphore_wait(barrier, 2 + can_up.astype(jnp.int32) + can_down.astype(jnp.int32))
    info_copy().start()
    middle_far_copy(1 - half_far).start()
    middle_near_copy().start()
    prepare_both(1)
    send_all(0)
    weigh_own(0)
    prepare_both(2)
    send_all(1)

    i, j = iotas((ups, wide))
    plane = (i * 205) >> 11
    parts_ref[0:ups] = ones_where((plane == (j >> 4)) & ((j & 15) >= i - plane * below + rows - below))
    i, j = iotas((downs, wide))
    plane = (i * 57) >> 9
    parts_ref[ups:] = ones_where((plane == (j >> 4)) & ((j & 15) <= i - plane * above))

    def build_window():
        i, j = iotas((wide, wide))
        inner_ref[...] = ones_where((i >> 4) == (j >> 4)) * ones_where((j - i <= above) & (i - j <= below))
        i, j = iotas((wide, ups))
        from_up_ref[...] = ones_where(((i & 15) < below) & (j == (i >> 4) * below + (i & 15)))
        i, j = iotas((wide, downs))
        from_down_ref[...] = ones_where(
            ((i & 15) >= rows - above) & (j == (i >> 4) * above + (i & 15) - (rows - above))
        )

    def meet_peer():
        weigh_own(1)
        info_copy().wait_recv()
        copy = pltpu.make_async_copy(info_in_ref, info_ref, info_sem)
        copy.start()
        peer_shifts = jnp.zeros((8, lanes), jnp.int32)
        for d in range(slots):
            peer_shifts = jnp.where(info_row == d, shift_of(info_in_ref[d : d + 1]), peer_shifts)
        for part, value in enumerate(make_taps(peer_shifts)):
            taps_ref[part, 8:16] = value
        weigh_peer()
        copy.wait()

    lane = lax.broadcasted_iota(jnp.int32, (rows, wide), 1) & (lanes - 1)
    from_before = ones_where(lane >= 64)
    from_after = ones_where(lane < 64)

    group = lax.broadcasted_iota(jnp.int32, (rows, lanes), 1) >> 5
    outer = (group == 0) | (group == 3)
    lower = group < 2
    even = (group & 1) == 0

    def pool(v):
        a = jnp.where(outer, v[0], v[2]) + pltpu.roll(jnp.where(outer, v[2], v[0]), 64, 1)
        b = jnp.where(lower, v[1], v[3]) + pltpu.roll(jnp.where(lower, v[3], v[1]), 64, 1)
        return jnp.where(even, a, b) + pltpu.roll(jnp.where(even, b, a), 32, 1)

    def make_edges(spot, ref, d, base):
        for q in range(tiles):
            edge_ref[spot, q] = ref[d, base + q - 1] * from_before + ref[d, base + q + 1] * from_after

    def tile_rows(ref, d, base):
        return ref[d, pl.ds(base, tiles)].reshape(tiles * rows, wide)

    def edge_rows(spot):
        return edge_ref[spot].reshape(tiles * rows, wide)

    def combine(pair, current, edges, weight, match, step):
        out = jnp.dot(
            jnp.concatenate(current, axis=0), weight_ref[weight, 0], preferred_element_type=jnp.float32
        )
        out = out + jnp.dot(
            jnp.concatenate(edges, axis=0), weight_ref[weight, 1], preferred_element_type=jnp.float32
        )
        band_ref[pair] = out
        for a in range(tiles // 4):
            sums = [[], [], [], []]
            for b in range(4):
                top = (4 * a + b) * rows
                fr, fi, sr, si = (
                    band_ref[
                        pair,
                        image * tiles * rows + top : image * tiles * rows + top + rows,
                        part * lanes : (part + 1) * lanes,
                    ]
                    for image in range(2)
                    for part in range(2)
                )
                sums[0].append(fr * sr + fi * si)
                sums[1].append(fi * sr - fr * si)
                sums[2].append(fr * fr + fi * fi)
                sums[3].append(sr * sr + si * si)
            for p in range(planes):
                top = (pair * planes + p) * rows
                looks_ref[match, step, top : top + rows, a * lanes : (a + 1) * lanes] = pool(sums[p]).astype(
                    jnp.bfloat16
                )

    def pass_on(match, step):
        parts = jnp.dot(parts_ref[...], looks_ref[match, step], preferred_element_type=jnp.float32)
        parts = parts.astype(jnp.bfloat16)

        @pl.when(can_up)
        def _():
            up_out_ref[match, step] = parts[0:ups]
            up_copy(match, step).start()

        @pl.when(can_down)
        def _():
            down_out_ref[match, step] = parts[ups:]
            down_copy(match, step).start()

    def compute_near(step):
        @pl.when(step == 0)
        def _():
            middle_near_copy().wait_recv()

        for half in range(2):
            near_copy(half, step).wait_recv()
        bases = [half * half_tiles + block_of(half, step) * tiles + 1 for half in range(2)]
        for half in range(2):
            for d in range(slots):
                make_edges(2 * slots * half + d, own_ref, d, bases[half])
                make_edges(2 * slots * half + slots + d, near_got_ref, d, bases[half])
        for half in range(2):
            for slot in range(slots):
                place = place_of(pairing_ref, 0, slot, slots)
                combine(
                    half * slots + slot,
                    [tile_rows(own_ref, place, bases[half]), tile_rows(near_got_ref, slot, bases[half])],
                    [edge_rows(2 * slots * half + place), edge_rows(2 * slots * half + slots + slot)],
                    slot,
                    0,
                    step,
                )

    def compute_far(step):
        @pl.when(step == 0)
        def _():
            middle_far_copy(half_far).wait_recv()

        @pl.when(step < blocks - 1)
        def _():
            far_copy(half_far, step).wait_recv()

        @pl.when(step == blocks - 1)
        def _():
            far_last_copy(half_far).wait_recv()

        got_base = block_of(half_far, step) * tiles + 1
        own_base = half_far * half_tiles + got_base
        for d in range(slots):
            make_edges(d, own_ref, d, own_base)
            make_edges(slots + d, far_got_ref, d, got_base)
        for pair in range(pairs):
            slot = pair % slots
            if pair < slots:
                place = place_of(pairing_ref, 1, slot, slots)
            else:
                place = partner_slot(info_ref[slot, 0], slots)
            current = [tile_rows(own_ref, place, own_base), tile_rows(far_got_ref, slot, got_base)]
            edges = [edge_rows(place), edge_rows(slots + slot)]
            if pair >= slots:
                current, edges = current[::-1], edges[::-1]
            combine(pair, current, edges, slots + pair, 1, step)

    def finish(match, step):
        @pl.when(can_down)
        def _():
            up_copy(match, step).wait_recv()

        @pl.when(can_up)
        def _():
            down_copy(match, step).wait_recv()

        window = jnp.dot(inner_ref[...], looks_ref[match, step], preferred_element_type=jnp.float32)
        window = window + jnp.dot(from_up_ref[...], up_in_ref[match, step], preferred_element_type=jnp.float32)
        window = window + jnp.dot(from_down_ref[...], down_in_ref[match, step], preferred_element_type=jnp.float32)
        window_ref[...] = window
        made = []
        for pair in range(pairs):
            cr, ci, pf, ps = (
                window_ref[(pair * planes + p) * rows : (pair * planes + p + 1) * rows] for p in range(planes)
            )
            made.append(
                [
                    (cr * (1.0 / 80.0)).astype(jnp.bfloat16),
                    (ci * (1.0 / 80.0)).astype(jnp.bfloat16),
                    (jnp.sqrt(cr * cr + ci * ci) * lax.rsqrt(pf * ps + epsilon)).astype(jnp.bfloat16),
                ]
            )
        places = [place_of(pairing_ref, match, slot, slots) for slot in range(slots)]

        def keep(own, half):
            for k in range(3):
                for d in range(slots):
                    value = own[0][k]
                    for slot in range(1, slots):
                        value = jnp.where(places[slot] == d, own[slot][k], value)
                    made_ref[match, d, k, :, columns_of(half, step)] = value

        @pl.when(match == 0)
        def _():
            for half in range(2):
                keep(made[half * slots : (half + 1) * slots], half)

        @pl.when(match == 1)
        def _():
            for d in range(slots):
                for k in range(3):
                    result_ref[step, d, k] = made[slots + d][k]
            result_copy(step, half_far).start()
            keep(made[:slots], half_far)

    steps = 2 * blocks

    @pl.when(jnp.logical_not(can_down))
    def _():
        up_in_ref[...] = jnp.zeros(up_in_ref.shape, up_in_ref.dtype)

    @pl.when(jnp.logical_not(can_up))
    def _():
        down_in_ref[...] = jnp.zeros(down_in_ref.shape, down_in_ref.dtype)

    def reached(t, bound):
        return (t + steps - bound) // steps

    def unit_of(t):
        odd = lax.rem(t, 2)
        first = 1 - reached(t, 1)
        late = reached(t, steps - 5)
        last = reached(t, steps - 2)
        middle = (1 - first) * (1 - late)
        match = middle * (1 - odd) + late * (1 - last)
        step = middle * ((t + odd) // 2 - (1 - odd)) + late * (1 - last) * (t - blocks + 2) + last * (t - blocks)
        return match, step

    def work_of(t):
        odd = lax.rem(t, 2)
        first = 1 - reached(t, 1)
        last = reached(t, steps - 1)
        match = (1 - odd) * (1 - first) + odd * last
        return match, odd * ((t + 1) // 2) + (1 - odd) * (1 - first) * (t // 2 - 1) - last

    def body(t, carry):
        match, step = work_of(t)

        @pl.when(match == 0)
        def _():
            compute_near(step)

            @pl.when(step < blocks - held)
            def _():
                pass_on(0, step)

        @pl.when(match == 1)
        def _():
            compute_far(step)
            pass_on(1, step)

        @pl.when(t + 3 < blocks)
        def _():
            prepare_both(t + 3)

        @pl.when(t + 2 < blocks)
        def _():
            send_all(t + 2)

        @pl.when(t == 1)
        def _():
            meet_peer()

        @pl.when(t == 2)
        def _():
            build_window()

        @pl.when(t == steps - 1)
        def _():
            for step in range(blocks - held, blocks):
                pass_on(0, step)

        @pl.when(t >= lag)
        def _():
            finish(*unit_of(jnp.maximum(t - lag, 0)))

        return carry

    lax.fori_loop(0, steps, body, 0)

    def rest(t, carry):
        finish(*unit_of(t))
        return carry

    lax.fori_loop(steps - lag, steps, rest, 0)

    def settle(step, carry):
        @pl.when(step < blocks - 1)
        def _():
            far_copy(1 - half_far, step).wait_send()

        @pl.when(step == blocks - 1)
        def _():
            far_last_copy(1 - half_far).wait_send()

        for half in range(2):
            near_copy(half, step).wait_send()
        for match in range(2):
            @pl.when(can_up)
            def _():
                up_copy(match, step).wait_send()

            @pl.when(can_down)
            def _():
                down_copy(match, step).wait_send()

        result_copy(step, half_far).wait_send()
        result_copy(step, 1 - half_far).wait_recv()
        return carry

    lax.fori_loop(0, blocks, settle, 0)
    info_copy().wait_send()
    middle_far_copy(1 - half_far).wait_send()
    middle_near_copy().wait_send()


def exchange(pairing, raw):
    slots, _, raw_rows, _ = raw.shape
    groups, strips = lax.axis_size("date"), lax.axis_size("strip")
    half_tiles = raw_rows // 4
    blocks = half_tiles // tiles
    pairs = 2 * slots
    wide = 2 * lanes
    size = tiles * lanes // 4
    ups, downs = pairs * planes * below, pairs * planes * above
    dma = pltpu.SemaphoreType.DMA
    return pl.pallas_call(
        lambda *refs: exchange_kernel(groups, strips, *refs),
        out_shape=jax.ShapeDtypeStruct((2, slots, 3, rows, 2 * blocks * size), jnp.bfloat16),
        in_specs=[pl.BlockSpec(memory_space=pltpu.SMEM), pl.BlockSpec(memory_space=pltpu.HBM)],
        out_specs=pl.BlockSpec(memory_space=pltpu.VMEM),
        scratch_shapes=[
            pltpu.VMEM(raw.shape, jnp.bfloat16),
            pltpu.VMEM((slots, 2 * half_tiles + 2, rows, wide), jnp.bfloat16),
            pltpu.VMEM((slots, 2 * half_tiles + 2, rows, wide), jnp.bfloat16),
            pltpu.VMEM((slots, half_tiles + 2, rows, wide), jnp.bfloat16),
            pltpu.VMEM((4 * slots, tiles, rows, wide), jnp.bfloat16),
            pltpu.VMEM((2, 16, lanes), jnp.float32),
            pltpu.VMEM((3 * slots, 2, wide, wide), jnp.bfloat16),
            pltpu.VMEM((pairs, 2 * tiles * rows, wide), jnp.float32),
            pltpu.VMEM((2, blocks, pairs * planes * rows, size), jnp.bfloat16),
            pltpu.VMEM((pairs * planes * rows, size), jnp.float32),
            pltpu.VMEM((2, blocks, ups, size), jnp.bfloat16),
            pltpu.VMEM((2, blocks, downs, size), jnp.bfloat16),
            pltpu.VMEM((2, blocks, ups, size), jnp.bfloat16),
            pltpu.VMEM((2, blocks, downs, size), jnp.bfloat16),
            pltpu.VMEM((blocks, slots, 3, rows, size), jnp.bfloat16),
            pltpu.VMEM((8, lanes), jnp.int32),
            pltpu.VMEM((8, lanes), jnp.int32),
            pltpu.SMEM((8, lanes), jnp.int32),
            pltpu.VMEM((wide, wide), jnp.bfloat16),
            pltpu.VMEM((wide, wide), jnp.bfloat16),
            pltpu.VMEM((ups + downs, wide), jnp.bfloat16),
            pltpu.VMEM((wide, ups), jnp.bfloat16),
            pltpu.VMEM((wide, downs), jnp.bfloat16),
            dma((2, blocks)),
            dma((2, blocks)),
            dma((2, blocks)),
            dma((blocks,)),
            dma((blocks,)),
            dma((2,)),
            dma((2,)),
            dma,
            dma,
            dma,
            dma((2, blocks)),
            dma((2, blocks)),
            dma((2, blocks)),
            dma((2, blocks)),
            dma((blocks,)),
            dma((blocks,)),
        ],
        compiler_params=pltpu.CompilerParams(
            vmem_limit_bytes=52000 << 10, collective_id=0, has_side_effects=True
        ),
        name="exchange",
    )(pairing, raw)


def hand_out_kernel(made_ref, cross_ref, coherence_ref, sem):
    copies = (
        pltpu.make_async_copy(made_ref.at[:, :, 0:2], cross_ref, sem.at[0]),
        pltpu.make_async_copy(made_ref.at[:, :, 2], coherence_ref, sem.at[1]),
    )
    for copy in copies:
        copy.start()
    for copy in copies:
        copy.wait()


def hand_out(made):
    matches, dates, _, count, columns = made.shape
    return pl.pallas_call(
        hand_out_kernel,
        out_shape=(
            jax.ShapeDtypeStruct((matches, dates, 2, count, columns), jnp.bfloat16),
            jax.ShapeDtypeStruct((matches, dates, count, columns), jnp.bfloat16),
        ),
        in_specs=[pl.BlockSpec(memory_space=pltpu.VMEM)],
        out_specs=[pl.BlockSpec(memory_space=pltpu.HBM)] * 2,
        scratch_shapes=[pltpu.SemaphoreType.DMA((2,))],
        compiler_params=pltpu.CompilerParams(vmem_limit_bytes=4 << 20),
        name="hand_out",
    )(made)


def per_device(acquisitions, partners, band_shifts):
    dates, count, _, samples = acquisitions.shape
    raw = acquisitions.reshape(dates, count, 2, samples // lanes, lanes)
    raw = raw.transpose(0, 1, 3, 2, 4).reshape(dates, count, 2 * (samples // lanes), lanes)
    return hand_out(exchange(partners * bins + band_shifts + bins // 2, raw))


def solution(mesh):
    in_specs = (
        P(("grp", "date"), "strip", None, None),
        P(None, ("grp", "date")),
        P(None, ("grp", "date")),
    )
    out_specs = (
        P(None, ("grp", "date"), None, "strip", None),
        P(None, ("grp", "date"), "strip", None),
    )
    return jax.shard_map(
        per_device, mesh=mesh, in_specs=in_specs, out_specs=out_specs, check_vma=False
    )
```
